32 devices in a mesh: layer: 4 (over x, core), lat: 8 (over z, y).
Axes of the slice: x: 2, y: 2, z: 4, core: 2. Of those that a mesh axis runs over, the one named last changes fastest.
Arguments:
- resid_in: bfloat16 [4, 4096, 256], P('layer', 'lat'), may hold values from -6 to 6
- resid_out: bfloat16 [4, 4096, 256], P('layer', 'lat'), may hold values from -80 to 80
- token_ids: int32 [256], replicated, may hold values from 0 to 128255, as said below
- active_mask: int32 [4, 6144, 256], P('layer', 'lat'), may hold values 0 or 1
- enc_weight: bfloat16 [4, 6144, 4096], P('layer', 'lat'), may hold values from -0.09375 to 0.09375
- enc_bias: bfloat16 [4, 6144], P('layer', 'lat'), may hold values from -3 to 3
- dec_weight: bfloat16 [4, 4, 6144, 4096], P('layer', None, 'lat'), may hold values from -0.078125 to 0.078125
- dec_bias: bfloat16 [4, 4096], P('layer', 'lat'), may hold values from -3 to 3
Outputs:
- enc_grad: bfloat16 [4, 6144, 4096], P('layer', 'lat')
- dec_grad: bfloat16 [4, 4, 6144, 4096], P('layer', None, 'lat')
- total_loss: float32 [], replicated
The draws below stay inside these ranges and needn't reach their ends.
Inputs may be any that keep to these rules, and one draw needn't show every extreme that they name: `token_ids`: ids of the Llama 3 vocabulary; the begin-of-text id 128000 stands at position 0 and at scattered other positions.
All inputs are finite; a program needn't handle non-finite values. No bound on the sum of `active_mask` on one device may be relied on, other than what follows from the above.
Results may differ from the reference program's by a relative error of at most 0.007.
Values may be sent and summed in bfloat16 or wider, within the bound.
A program may use at most 128 MiB of HBM per device.

```python
import math
import jax
import jax.numpy as jnp

D = 4096
M = 6144
TOK = 256
L = 4


def draw_token_ids(key, part):
    first_key, second_key = jax.random.split(jax.random.fold_in(key, 11))
    token_list = jax.random.randint(first_key, (TOK,), 0, 128256, dtype=jnp.int32)
    starting = jax.random.randint(second_key, (TOK,), 0, 8, dtype=jnp.int32) == 0
    token_list = jnp.where(starting, jnp.int32(128000), token_list)
    return token_list.at[0].set(jnp.int32(128000))


def draw_resid_out(key, part):
    base_key, feature_key, token_key = jax.random.split(jax.random.fold_in(key, 23), 3)
    base_values = jax.random.truncated_normal(base_key, -4.0, 4.0, (L, D, TOK), jnp.float32)
    feature_scale = jnp.exp(jax.random.uniform(feature_key, (L, D, 1), jnp.float32, 0.0, math.log(10.0)))
    token_scale = jnp.exp(jax.random.uniform(token_key, (1, 1, TOK), jnp.float32, 0.0, math.log(2.0)))
    return (base_values * feature_scale * token_scale).astype(jnp.bfloat16)


def plant(drawn, stream_key, low, largest):
    spot = [jax.random.randint(jax.random.fold_in(stream_key, axis), (), 0, length) for axis, length in enumerate(drawn.shape)]
    main_axis = drawn.shape.index(max(drawn.shape))
    next_to = spot[:main_axis] + [(spot[main_axis] + 1) % drawn.shape[main_axis]] + spot[main_axis + 1:]
    return drawn.at[tuple(spot)].set(low).at[tuple(next_to)].set(largest)


def levels(own_key, extent, shards, least, top_value):
    def one(position, blocks):
        steps = jax.random.uniform(jax.random.fold_in(jax.random.fold_in(own_key, 6), position), (blocks,), jnp.float32, least / len(shards), top_value / len(shards))
        return jnp.repeat(jnp.exp(steps), extent[position] // blocks).reshape((-1,) + (1,) * (len(extent) - position - 1))

    factor_of = one(*shards[0])
    for cut in shards[1:]:
        factor_of = factor_of * one(*cut)
    return factor_of


def normal_values(stream_key, dims, width, reach, cuts=(), kind=jnp.bfloat16):
    level = levels(stream_key, dims, cuts, -0.22, 0.18) if cuts else 1.0
    values = jax.random.normal(stream_key, dims, jnp.float32) * width * level
    return jnp.minimum(jnp.maximum(values, -reach), reach).astype(kind)


def setup_inputs(seed: int = 0) -> dict:
    splits = jax.random.split(jax.random.key(seed), 9)
    return {
        "resid_in": normal_values(splits[0], (L, D, TOK), 1.0, 6.0, ((0, 4), (1, 8))),
        "resid_out": draw_resid_out(jax.random.fold_in(splits[8], 71), 0),
        "token_ids": draw_token_ids(jax.random.fold_in(splits[8], 71), 0),
        "active_mask": plant((jax.random.randint(splits[3], (L, M, TOK), 0, 2) < 1).astype(jnp.int32), jax.random.fold_in(splits[3], 1), 0, 1),
        "enc_weight": normal_values(splits[4], (L, M, D), D ** -0.5, 0.09375, ((0, 4), (1, 8))),
        "enc_bias": normal_values(splits[5], (L, M), 0.5, 3.0, ((0, 4), (1, 8))),
        "dec_weight": normal_values(splits[6], (L, L, M, D), M ** -0.5, 0.078125, ((0, 4), (2, 8))),
        "dec_bias": normal_values(splits[7], (L, D), 0.5, 3.0, ((0, 4), (1, 8))),
    }


EPSILON = 1e-5


def reference(resid_in, resid_out, token_ids, active_mask, enc_weight, enc_bias, dec_weight, dec_bias):
    kept_tokens = (token_ids != 128000).astype(jnp.float32)
    latents = []
    gatings = []
    for layer in range(L):
        preact = jnp.dot(enc_weight[layer], resid_in[layer], preferred_element_type=jnp.float32)
        preact = preact + enc_bias[layer].astype(jnp.float32)[:, None]
        gating = active_mask[layer].astype(jnp.float32)
        gatings.append(gating)
        latents.append((gating * preact).astype(jnp.bfloat16))
    total_cells = D * TOK
    total_loss = jnp.zeros((), jnp.float32)
    out_grads = []
    for target in range(L):
        recon = jnp.zeros((D, TOK), jnp.float32) + dec_bias[target].astype(jnp.float32)[:, None]
        for source in range(target + 1):
            recon = recon + jnp.dot(dec_weight[target, source].T, latents[source], preferred_element_type=jnp.float32)
        wanted = resid_out[target].astype(jnp.float32)
        centered = wanted - jnp.mean(wanted, axis=1, keepdims=True)
        spread = jnp.sum(centered * centered) / total_cells + EPSILON
        residual_err = kept_tokens[None, :] * (recon - wanted)
        total_loss = total_loss + jnp.sum(residual_err * residual_err) / (2.0 * spread * total_cells)
        out_grads.append((residual_err / spread).astype(jnp.bfloat16))
    enc_rows = []
    for source in range(L):
        latent_grad = jnp.zeros((M, TOK), jnp.float32)
        for target in range(source, L):
            latent_grad = latent_grad + jnp.dot(dec_weight[target, source], out_grads[target], preferred_element_type=jnp.float32)
        preact_grad = (gatings[source] * latent_grad).astype(jnp.bfloat16)
        enc_rows.append(jnp.dot(preact_grad, resid_in[source].T, preferred_element_type=jnp.float32).astype(jnp.bfloat16))
    enc_grad = jnp.stack(enc_rows)
    dec_rows = []
    for target in range(L):
        row_list = []
        for source in range(L):
            if source <= target:
                row_list.append(jnp.dot(latents[source], out_grads[target].T, preferred_element_type=jnp.float32).astype(jnp.bfloat16))
            else:
                row_list.append(jnp.zeros((M, D), jnp.bfloat16))
        dec_rows.append(jnp.stack(row_list))
    dec_grad = jnp.stack(dec_rows)
    return enc_grad, dec_grad, total_loss
```

```python
import functools

import jax
import jax.numpy as jnp
from jax import lax
from jax.experimental import pallas as pl
from jax.experimental.pallas import tpu as pltpu
from jax.sharding import PartitionSpec as P

EPSILON = 1e-05
F32 = jnp.float32
BF16 = jnp.bfloat16


class Place:
    def __init__(self, lat_count):
        self.me = lax.axis_index("lat")
        self.depth = lat_count // 2
        self.z = self.me // 2
        self.y = self.me % 2
        self.partner = self.me + 1 - 2 * self.y
        self.has_up = self.z < self.depth - 1
        self.has_down = self.z > 0


def send(src, dst, send_sem, recv_sem, lat):
    return pltpu.make_async_remote_copy(
        src_ref=src,
        dst_ref=dst,
        send_sem=send_sem,
        recv_sem=recv_sem,
        device_id={"lat": lat},
        device_id_type=pl.DeviceIdType.MESH,
    )


def greet(at, more=0):
    barrier = pltpu.get_barrier_semaphore()

    def hello(lat):
        pl.semaphore_signal(
            barrier, inc=1, device_id={"lat": lat}, device_id_type=pl.DeviceIdType.MESH
        )

    hello(at.partner)
    pl.when(at.has_up)(lambda: hello(at.me + 2))
    pl.when(at.has_down)(lambda: hello(at.me - 2))
    peers = 1 + more + at.has_up.astype(jnp.int32) + at.has_down.astype(jnp.int32)
    pl.semaphore_wait(barrier, peers)


class Gather:
    def __init__(self, at, own, whole, sems):
        self.at, self.own, self.whole, self.sems = at, own, whole, sems

    def hop(self, kind, d):
        at = self.at
        shard = at.me - 2 * d if kind in (0, 2) else at.me + 2 * d
        src = self.own if d == 0 else self.whole.at[shard]
        to = (at.me + 2, at.me - 2, at.partner, at.partner)[kind]
        later = d + 1 if kind < 2 else d
        return send(
            src, self.whole.at[shard], self.sems.at[0, kind, d], self.sems.at[1, kind, later], to
        )

    def landing(self, kind, d):
        at = self.at
        below = kind in (0, 2)
        shard = at.me - 2 * d if below else at.me + 2 * d
        if kind >= 2:
            shard = shard + 1 - 2 * at.y
        ref = self.whole.at[shard]
        return send(ref, ref, self.sems.at[0, kind, d], self.sems.at[1, kind, d], at.partner)

    def start(self):
        pl.when(self.at.has_up)(lambda: self.hop(0, 0).start())
        pl.when(self.at.has_down)(lambda: self.hop(1, 0).start())
        self.hop(2, 0).start()

    def step(self, d):
        at = self.at

        @pl.when(at.z >= d)
        def _():
            self.landing(0, d).wait_recv()
            pl.when(at.has_up)(lambda: self.hop(0, d).start())
            self.hop(2, d).start()

        @pl.when(at.z + d < at.depth)
        def _():
            self.landing(1, d).wait_recv()
            pl.when(at.has_down)(lambda: self.hop(1, d).start())
            self.hop(3, d).start()

    def finish(self, crossed=False):
        at = self.at
        for d in range(at.depth):

            @pl.when(at.z >= d)
            def _():
                if not crossed:
                    self.landing(2, d).wait_recv()
                self.hop(2, d).wait_send()
                if d < at.depth - 1:
                    pl.when(at.has_up)(lambda: self.hop(0, d).wait_send())

            @pl.when(at.z + d < at.depth)
            def _():
                if d > 0:
                    if not crossed:
                        self.landing(3, d).wait_recv()
                    self.hop(3, d).wait_send()
                if d < at.depth - 1:
                    pl.when(at.has_down)(lambda: self.hop(1, d).wait_send())


def gather_kernel(lat_count, own, wanted_ref, whole, stats, stat, big_sems, stat_sems, local_sem):
    at = Place(lat_count)
    greet(at)
    big = Gather(at, own, whole, big_sems)
    big.start()
    keep = pltpu.make_async_copy(own, whole.at[at.me], local_sem)
    keep.start()
    wanted = wanted_ref[...].astype(F32)
    centered = wanted - jnp.mean(wanted, axis=1, keepdims=True)
    total = jnp.sum(centered * centered, keepdims=True)
    stat[...] = jnp.broadcast_to(total, stat.shape)
    stats[at.me] = stat[...]
    small = Gather(at, stat, stats, stat_sems)
    small.start()
    for d in range(1, at.depth):
        big.step(d)
        small.step(d)
    keep.wait()
    big.finish()
    small.finish()


def reduce_kernel(
    lat_count,
    parts,
    wanted_ref,
    bias_ref,
    kept_ref,
    spread_ref,
    whole,
    stats,
    across_up,
    across_down,
    from_below,
    from_above,
    going_up,
    going_down,
    total,
    grad,
    stat,
    across_sems,
    line_sems,
    big_sems,
    stat_sems,
):
    at = Place(lat_count)
    depth = at.depth
    greet(at)

    def across(up, d):
        rung = at.z + d if up else at.z - d
        row = 0 if up else 1
        return send(
            parts.at[rung * 2 + 1 - at.y],
            (across_up if up else across_down).at[d],
            across_sems.at[0, row, d],
            across_sems.at[1, row, d],
            at.partner,
        )

    def along(up, d):
        row = 0 if up else 1
        return send(
            (going_up if up else going_down).at[d],
            (from_below if up else from_above).at[d - 1],
            line_sems.at[0, row, d],
            line_sems.at[1, row, d - 1],
            at.me + 2 if up else at.me - 2,
        )

    def arrived(up, d):
        row = 0 if up else 1
        ref = (from_below if up else from_above).at[d]
        send(ref, ref, line_sems.at[0, row, d], line_sems.at[1, row, d], at.partner).wait_recv()

    for d in range(depth - 1, -1, -1):
        pl.when(at.z + d < depth)(lambda: across(True, d).start())
        if d:
            pl.when(at.z >= d)(lambda: across(False, d).start())

    def forward(up, d):
        across(up, d).wait_recv()
        rung = at.z + d if up else at.z - d
        crossed = across_up if up else across_down
        came = from_below if up else from_above
        going = going_up if up else going_down
        behind = at.has_down if up else at.has_up
        mine = parts.at[rung * 2 + at.y]

        @pl.when(behind)
        def _():
            if d < depth - 1:
                arrived(up, d)
                going[d] = (
                    mine[...].astype(F32) + crossed[d].astype(F32) + came[d].astype(F32)
                ).astype(BF16)

        @pl.when(jnp.logical_not(behind))
        def _():
            going[d] = (mine[...].astype(F32) + crossed[d].astype(F32)).astype(BF16)

        along(up, d).start()

    for d in range(depth - 1, 0, -1):
        pl.when(at.z + d < depth)(lambda: forward(True, d))
        pl.when(at.z >= d)(lambda: forward(False, d))
    across(True, 0).wait_recv()
    total[...] = (
        parts[at.me].astype(F32)
        + across_up[0].astype(F32)
        + (bias_ref[...] - wanted_ref[...].astype(F32))
    )

    @pl.when(at.has_down)
    def _():
        arrived(True, 0)
        total[...] += from_below[0].astype(F32)

    @pl.when(at.has_up)
    def _():
        arrived(False, 0)
        total[...] += from_above[0].astype(F32)

    err = kept_ref[...] * total[...]
    grad[...] = (err / spread_ref[...]).astype(BF16)
    whole[at.me] = grad[...]
    big = Gather(at, grad, whole, big_sems)
    big.start()
    stat[...] = jnp.broadcast_to(jnp.sum(err * err, keepdims=True), stat.shape)
    stats[at.me] = stat[...]
    small = Gather(at, stat, stats, stat_sems)
    small.start()
    for d in range(1, depth):
        big.step(d)
        small.step(d)
    big.finish()
    small.finish()
    for d in range(depth - 1, -1, -1):

        @pl.when(at.z + d < depth)
        def _():
            across(True, d).wait_send()
            if d:
                along(True, d).wait_send()

        if d:

            @pl.when(at.z >= d)
            def _():
                across(False, d).wait_send()
                along(False, d).wait_send()


def to_layer(src, dst, send_sem, recv_sem, layer):
    return pltpu.make_async_remote_copy(
        src_ref=src,
        dst_ref=dst,
        send_sem=send_sem,
        recv_sem=recv_sem,
        device_id={"layer": layer},
        device_id_type=pl.DeviceIdType.MESH,
    )


class Spread:
    def __init__(self, at, ref, sems, pair_sems):
        self.at, self.ref, self.sems, self.pair_sems = at, ref, sems, pair_sems

    def shard_of(self, kind, d, landing=False):
        at = self.at
        shard = at.me - 2 * d if kind in (0, 2) else at.me + 2 * d
        if landing and kind >= 2:
            shard = shard + 1 - 2 * at.y
        return shard

    def hop(self, kind, d):
        at = self.at
        ref = self.ref(self.shard_of(kind, d))
        later = d + 1 if kind < 2 else d
        to = (at.me + 2, at.me - 2, at.partner, at.partner)[kind]
        return send(ref, ref, self.sems.at[0, kind, d], self.sems.at[1, kind, later], to)

    def landing(self, kind, d):
        ref = self.ref(self.shard_of(kind, d, True))
        return send(
            ref, ref, self.sems.at[0, kind, d], self.sems.at[1, kind, d], self.at.partner
        )

    def crossing(self, what, kind, d, act):
        if d != 1 or self.pair_sems is None:
            act(what(kind, d))
            return
        straight = jnp.logical_not(self.at.odd) if kind == 2 else self.at.odd
        pl.when(straight)(lambda: act(what(kind, d)))

    def aside(self, landing=False):
        at = self.at
        ref = self.ref(at.beside + 1 - 2 * at.y if landing else at.partner)
        return send(ref, ref, self.pair_sems.at[0], self.pair_sems.at[1], at.beside)

    def start(self):
        self.hop(2, 0).start()
        pl.when(self.at.has_up)(lambda: self.hop(0, 0).start())
        pl.when(self.at.has_down)(lambda: self.hop(1, 0).start())

    def line(self, d):
        at = self.at

        @pl.when(at.z >= d)
        def _():
            self.landing(0, d).wait_recv()
            pl.when(at.has_up)(lambda: self.hop(0, d).start())
            self.crossing(self.hop, 2, d, lambda one: one.start())

        @pl.when(at.z + d < at.depth)
        def _():
            self.landing(1, d).wait_recv()
            pl.when(at.has_down)(lambda: self.hop(1, d).start())
            self.crossing(self.hop, 3, d, lambda one: one.start())

    def settle(self, d):
        at = self.at
        if d == 0:
            self.landing(2, 0).wait_recv()
            if self.pair_sems is not None:
                self.aside().start()
            return
        if d == 1 and self.pair_sems is not None:
            self.aside(True).wait_recv()
        arrive = lambda one: one.wait_recv()
        pl.when(at.z >= d)(lambda: self.crossing(self.landing, 2, d, arrive))
        pl.when(at.z + d < at.depth)(lambda: self.crossing(self.landing, 3, d, arrive))

    def finish(self):
        at = self.at
        if self.pair_sems is not None:
            self.aside().wait_send()
        for d in range(at.depth):

            @pl.when(at.z >= d)
            def _():
                self.crossing(self.hop, 2, d, lambda one: one.wait_send())
                if d < at.depth - 1:
                    pl.when(at.has_up)(lambda: self.hop(0, d).wait_send())

            @pl.when(at.z + d < at.depth)
            def _():
                if d > 0:
                    self.crossing(self.hop, 3, d, lambda one: one.wait_send())
                if d < at.depth - 1:
                    pl.when(at.has_down)(lambda: self.hop(1, d).wait_send())


def advance(at, group, d, use, before_last=None):
    if d < at.depth:
        for one in group:
            one.line(d)
    if d == 1:
        use(at.me)
    if d < at.depth:
        pl.when(at.z >= d)(lambda: use(at.me - 2 * d))
        pl.when(at.z + d < at.depth)(lambda: use(at.me + 2 * d))
    for one in group:
        one.settle(d - 1)
    if before_last is not None:
        before_last()
    pl.when(at.z >= d - 1)(lambda: use(at.partner - 2 * (d - 1)))
    if d > 1:
        pl.when(at.z + d - 1 < at.depth)(lambda: use(at.partner + 2 * (d - 1)))


class Tally:
    def __init__(self, at, lat_count, stats, sems):
        self.at, self.lat_count, self.stats, self.sems = at, lat_count, stats, sems

    def message(self, k, landing=False):
        me, count = self.at.me, self.lat_count
        ref = self.stats.at[lax.rem(me + count - k, count) if landing else me]
        return send(ref, ref, self.sems.at[0, k], self.sems.at[1, k], lax.rem(me + k, count))

    def start(self, value):
        self.stats[self.at.me] = jnp.broadcast_to(value, self.stats.shape[1:])
        for k in range(1, self.lat_count):
            self.message(k).start()

    def total(self):
        for k in range(1, self.lat_count):
            self.message(k, True).wait_recv()
            self.message(k).wait_send()
        return jnp.sum(self.stats[...], axis=0)


def step_kernel(
    lat_count,
    own,
    wanted_ref,
    enc_weight,
    enc_bias,
    gate_ref,
    dec_weight,
    dec_bias,
    ids_ref,
    turned_x_out,
    grads_out,
    acts_out,
    own_term_out,
    terms_out,
    loss,
    whole_x,
    turned_x,
    wanted_here,
    gate_here,
    enc_blocks,
    acc_enc,
    acts,
    turned,
    blocks,
    base,
    kept,
    leaving,
    crossed,
    came,
    going,
    pair_in,
    fresh,
    fresh_half,
    whole_g,
    column,
    acc,
    giving,
    given,
    terms,
    losses,
    spread_tile,
    stats,
    x_sems,
    x_pair_sems,
    g_sems,
    g_pair_sems,
    across_sems,
    line_sems,
    pair_sems,
    layer_sems,
    mate_sems,
    loss_sems,
    stat_sems,
    enc_sems,
    block_sems,
    local_sems,
    out_sems,
):
    at = Place(lat_count)
    at.odd = at.z % 2 == 1
    at.beside = at.me + 2 - 4 * (at.z % 2)
    depth = at.depth
    layer_count = acts.shape[1]
    rows, half = whole_x.shape[2:]
    piece = half // 2
    layer = lax.axis_index("layer")
    pairs = layer_count // 2
    pair, core = layer // 2, layer % 2
    mate = layer + 1 - 2 * core
    cells = lat_count * rows * half * 2

    def own_half(h):
        return pltpu.make_async_copy(
            own.at[:, pl.ds(h * half, half)], whole_x.at[h, at.me], local_sems.at[h]
        )

    def load_enc(g):
        return pltpu.make_async_copy(
            enc_weight.at[:, pl.ds(g * rows, rows)], enc_blocks.at[g], enc_sems.at[g]
        )

    def load_dec(g):
        return pltpu.make_async_copy(
            dec_weight.at[:, :, pl.ds(g * rows, rows)], blocks.at[g], block_sems.at[g]
        )

    fetch = pltpu.make_async_copy(wanted_ref, wanted_here, local_sems.at[2])
    fetch_gate = pltpu.make_async_copy(gate_ref, gate_here, local_sems.at[3])
    own_half(0).start()
    own_half(1).start()
    for g in range(lat_count):
        load_enc(g).start()
    fetch.start()
    fetch_gate.start()

    barrier = pltpu.get_barrier_semaphore()
    for k in range(1, layer_count):
        other = lax.rem(layer + k, layer_count)
        pl.semaphore_signal(
            barrier, inc=1, device_id={"layer": other}, device_id_type=pl.DeviceIdType.MESH
        )
    own_half(0).wait()
    own_half(1).wait()
    for k in range(1, lat_count):
        pl.semaphore_signal(
            barrier,
            inc=1,
            device_id={"lat": lax.rem(at.me + k, lat_count)},
            device_id_type=pl.DeviceIdType.MESH,
        )
    pl.semaphore_wait(barrier, layer_count + lat_count - 2)

    def feature_piece(h, q):
        def ref(shard):
            return whole_x.at[h, shard, pl.ds(q * (rows // 2), rows // 2)]

        return Spread(at, ref, x_sems.at[h, q], x_pair_sems.at[h] if q else None)

    def use_x(h):
        def use(g):
            acc_enc[h] += jnp.dot(enc_blocks[g], whole_x[h, g], preferred_element_type=F32)
            turned_x[g, h * half : (h + 1) * half] = jnp.transpose(whole_x[h, g])

        return use

    gather_x = [[feature_piece(h, q) for q in range(2)] for h in range(2)]

    def start_x(h):
        for one in gather_x[h]:
            one.start()

    def stage_x(h, d):
        advance(at, gather_x[h], d, use_x(h))

    start_x(0)
    bias = jnp.transpose(jnp.broadcast_to(enc_bias[...].astype(F32), (half, enc_bias.shape[1])))
    acc_enc[0] = bias
    acc_enc[1] = bias
    for g in range(lat_count):
        load_enc(g).wait()
    for g in range(lat_count):
        load_dec(g).start()
    stage_x(0, 1)
    start_x(1)
    fetch.wait()
    wanted = wanted_here[...].astype(F32)
    centered = wanted - jnp.mean(wanted, axis=1, keepdims=True)
    spread_tally = Tally(at, lat_count, stats.at[0], stat_sems.at[0])
    spread_tally.start(jnp.sum(centered * centered, keepdims=True))
    stage_x(0, 2)
    stage_x(1, 1)
    base[...] = dec_bias[...].astype(F32) - jnp.transpose(wanted_here[...].astype(F32))
    stage_x(0, 3)
    stage_x(1, 2)
    stage_x(0, 4)
    fetch_gate.wait()

    def over(h, k):
        ref = acts.at[h, layer]
        return to_layer(
            ref, ref, layer_sems.at[0, h, 0, k], layer_sems.at[1, h, 0, k], layer + 2 * k
        )

    def pass_on(h, k):
        ref = acts.at[h, layer - 2 * k]
        return to_layer(ref, ref, layer_sems.at[0, h, 1, k], layer_sems.at[1, h, 1, k], mate)

    def landed(h, kind, k):
        ref = acts.at[h, layer - 2 * k if kind == 0 else mate - 2 * k]
        sem = layer_sems.at[1, h, kind, k]
        return to_layer(ref, ref, layer_sems.at[0, h, kind, k], sem, mate)

    def turn(h, source):
        turned[source, h * half : (h + 1) * half] = jnp.transpose(acts[h, source])

    def exchange(h):
        gate = gate_here[:, h * half : (h + 1) * half].astype(F32)
        acts[h, layer] = (gate * acc_enc[h]).astype(BF16)
        for k in range(1, pairs):
            pl.when(pair + k < pairs)(lambda: over(h, k).start())
        pl.when(core == 0)(lambda: pass_on(h, 0).start())
        turn(h, layer)
        yield
        for k in range(1, pairs):

            @pl.when(pair >= k)
            def _():
                landed(h, 0, k).wait_recv()
                pass_on(h, k).start()
                turn(h, layer - 2 * k)

        yield

        @pl.when(core == 1)
        def _():
            landed(h, 1, 0).wait_recv()
            turn(h, mate)

        for k in range(1, pairs):

            @pl.when(pair >= k)
            def _():
                landed(h, 1, k).wait_recv()
                turn(h, mate - 2 * k)

        yield

    def exchange_sent(h):
        pl.when(core == 0)(lambda: pass_on(h, 0).wait_send())
        for k in range(1, pairs):
            pl.when(pair >= k)(lambda: pass_on(h, k).wait_send())
            pl.when(pair + k < pairs)(lambda: over(h, k).wait_send())

    moves = [exchange(h) for h in range(2)]
    next(moves[0])
    stage_x(1, 3)
    next(moves[0])
    stage_x(1, 4)
    next(moves[1])
    next(moves[0])
    for g in range(lat_count):
        load_dec(g).wait()
    spread_tile[...] = spread_tally.total() / cells + EPSILON
    spread = jnp.max(spread_tile[...], keepdims=True)

    def part(g, h=None):
        into = fresh if h is None else fresh_half
        some = slice(None) if h is None else slice(h * half, (h + 1) * half)
        into[...] = jnp.dot(turned[0, some], blocks[g, 0], preferred_element_type=F32)

        @pl.loop(1, layer + 1)
        def _(source):
            into[...] += jnp.dot(
                turned[source, some], blocks[g, source], preferred_element_type=F32
            )

    def of(p):
        return pl.ds(p * piece, piece)

    def across(p, up, d):
        row = 0 if up else 1
        return send(
            leaving.at[row, d, of(p)],
            crossed.at[row, d, of(p)],
            across_sems.at[0, p, row, d],
            across_sems.at[1, p, row, d],
            at.partner,
        )

    def aside(p, up):
        return send(
            leaving.at[0 if up else 1, 1, of(p)],
            pair_in.at[p // 2],
            pair_sems.at[0, p // 2],
            pair_sems.at[1, p // 2],
            at.beside,
        )

    def by_side(p, up, d, cross, turn_aside=None):
        if d != 1 or p % 2 == 0:
            cross()
            return
        beside = jnp.logical_not(at.odd) if up else at.odd
        pl.when(jnp.logical_not(beside))(cross)
        if turn_aside is not None:
            pl.when(beside)(turn_aside)

    def along(p, up, d):
        row = 0 if up else 1
        return send(
            going.at[row, d, of(p)],
            came.at[row, d - 1, of(p)],
            line_sems.at[0, p, row, d],
            line_sems.at[1, p, row, d - 1],
            at.me + 2 if up else at.me - 2,
        )

    def arrived(p, up, d):
        row = 0 if up else 1
        ref = came.at[row, d, of(p)]
        sems = line_sems.at[0, p, row, d], line_sems.at[1, p, row, d]
        send(ref, ref, *sems, at.partner).wait_recv()
        fresh[of(p), :] += came[row, d, of(p)].astype(F32)

    def met(p, up, d):
        across(p, up, d).wait_recv()
        fresh[of(p), :] += crossed[0 if up else 1, d, of(p)].astype(F32)

    def leave(h, up, d):
        row = 0 if up else 1
        part(at.partner + 2 * d if up else at.partner - 2 * d, h)
        if d == 0:
            aside(2 * h + 1, True).wait_recv()
            fresh_half[piece:] += pair_in[h].astype(F32)
        leaving[row, d, h * half : (h + 1) * half] = fresh_half[...].astype(BF16)
        for p in (2 * h, 2 * h + 1):
            by_side(
                p, up, d, lambda: across(p, up, d).start(), lambda: aside(p, up).start()
            )

    def leaves(h, d):
        pl.when(at.z + d < depth)(lambda: leave(h, True, d))
        if d:
            pl.when(at.z >= d)(lambda: leave(h, False, d))

    def forward(up, d):
        row = 0 if up else 1
        part(at.me + 2 * d if up else at.me - 2 * d)
        for p in range(4):
            by_side(p, up, d, lambda: met(p, up, d))
            if d < depth - 1:
                pl.when(at.has_down if up else at.has_up)(lambda: arrived(p, up, d))
            going[row, d, of(p)] = fresh[of(p), :].astype(BF16)
            along(p, up, d).start()

    def forwards(d):
        pl.when(at.z + d < depth)(lambda: forward(True, d))
        pl.when(at.z >= d)(lambda: forward(False, d))

    def token_piece(p):
        def ref(shard):
            return whole_g.at[shard, of(p)]

        return Spread(at, ref, g_sems.at[p], g_pair_sems.at[p // 2] if p % 2 else None)

    gather_g = [token_piece(p) for p in range(4)]

    def use_g(g):
        column[...] = jnp.transpose(whole_g[g])

        @pl.loop(0, layer + 1)
        def _(source):
            acc[source] += jnp.dot(blocks[g, source], column[...], preferred_element_type=F32)

    def close(p):
        met(p, True, 0)
        pl.when(at.has_down)(lambda: arrived(p, True, 0))
        pl.when(at.has_up)(lambda: arrived(p, False, 0))
        err = kept[of(p), :1] * fresh[of(p), :]
        whole_g[at.me, of(p)] = (err / spread).astype(BF16)
        gather_g[p].start()
        fresh[of(p), :] = err * err

    leaves(0, 3)
    next(moves[1])
    leaves(0, 2)
    leaves(0, 1)
    next(moves[1])
    leaves(1, 3)
    forwards(3)
    leaves(1, 2)
    leaves(1, 1)
    forwards(2)
    leaves(0, 0)
    leaves(1, 0)
    forwards(1)
    ids = jnp.broadcast_to((ids_ref[...] != 128000).astype(F32), (128, 2 * half))
    kept[...] = jnp.transpose(ids)
    part(at.me)
    fresh[...] += base[...]
    for p in range(4):
        close(p)
    err_tally = Tally(at, lat_count, stats.at[1], stat_sems.at[1])
    err_tally.start(jnp.sum(fresh[...], keepdims=True))
    acc[...] = jnp.zeros_like(acc)
    advance(at, gather_g, 1, use_g)
    advance(at, gather_g, 2, use_g)
    advance(at, gather_g, 3, use_g)

    def out(which):
        src, dst = (
            (turned_x, turned_x_out),
            (acts, acts_out),
            (whole_g, grads_out),
            (acc.at[layer], own_term_out),
            (terms, terms_out),
        )[which]
        return pltpu.make_async_copy(src, dst, out_sems.at[which])

    out(0).start()
    out(1).start()
    advance(at, gather_g, 4, use_g, lambda: out(2).start())
    losses[layer] = err_tally.total() / (2.0 * spread_tile[...] * cells)

    def tell(k, told=False):
        other = lax.rem(layer + (layer_count - k if told else k), layer_count)
        ref = losses.at[other if told else layer]
        return to_layer(ref, ref, loss_sems.at[0, k], loss_sems.at[1, k], other)

    def give(k):
        return to_layer(
            giving.at[k], given.at[k], mate_sems.at[0, k], mate_sems.at[1, k], mate
        )

    def hand(k):
        giving[k] = acc[mate - 2 * k].astype(BF16)
        give(k).start()

    for k in range(pairs - 1, 0, -1):
        pl.when(pair >= k)(lambda: hand(k))
    pl.when(core == 1)(lambda: hand(0))
    for k in range(1, layer_count):
        tell(k).start()
    for k in range(pairs - 1, 0, -1):

        @pl.when(pair >= k)
        def _():
            give(k).wait_recv()
            terms[k - 1] = (acc[layer - 2 * k] + given[k].astype(F32)).astype(BF16)
            give(k).wait_send()

        @pl.when(pair < k)
        def _():
            terms[k - 1] = jnp.zeros(terms.shape[1:], BF16)

    out(4).start()

    @pl.when(core == 0)
    def _():
        give(0).wait_recv()
        acc[layer] += given[0].astype(F32)

    out(3).start()
    pl.when(core == 1)(lambda: give(0).wait_send())
    for k in range(1, layer_count):
        tell(k, True).wait_recv()
        tell(k).wait_send()
    loss[...] = jnp.sum(losses[...], axis=0)[:1, :1]
    for h in range(2):
        for one in gather_x[h]:
            one.finish()
        exchange_sent(h)
    for one in gather_g:
        one.finish()
    for p in range(4):
        if p % 2:
            aside(p, True).wait_send()
        for d in range(depth):
            for up in (True, False):
                if d or up:

                    @pl.when(at.z + d < depth if up else at.z >= d)
                    def _():
                        by_side(p, up, d, lambda: across(p, up, d).wait_send())
                        if d:
                            along(p, up, d).wait_send()

    for which in range(5):
        out(which).wait()


VMEM = pl.BlockSpec(memory_space=pltpu.VMEM)
HBM = pl.BlockSpec(memory_space=pltpu.HBM)


def step(inputs_local, wanted, enc_weight, enc_bias, gate, dec_weight, dec_bias, ids, lat_count):
    rows, tokens = inputs_local.shape
    layer_count, lat_rows, _ = dec_weight.shape
    depth = lat_count // 2
    pairs = layer_count // 2
    half = tokens // 2
    slots = pltpu.VMEM((2, depth, tokens, rows), BF16)
    dma = pltpu.SemaphoreType.DMA
    return pl.pallas_call(
        functools.partial(step_kernel, lat_count),
        out_shape=(
            jax.ShapeDtypeStruct((lat_count, tokens, rows), BF16),
            jax.ShapeDtypeStruct((lat_count, tokens, rows), BF16),
            jax.ShapeDtypeStruct((2, layer_count, lat_rows, half), BF16),
            jax.ShapeDtypeStruct((lat_rows, tokens), F32),
            jax.ShapeDtypeStruct((pairs - 1, lat_rows, tokens), BF16),
            jax.ShapeDtypeStruct((1, 1), F32),
        ),
        in_specs=[HBM, HBM, HBM, VMEM, HBM, HBM, VMEM, VMEM],
        out_specs=(HBM,) * 5 + (VMEM,),
        scratch_shapes=[
            pltpu.VMEM((2, lat_count, rows, half), BF16),
            pltpu.VMEM((lat_count, tokens, rows), BF16),
            pltpu.VMEM((rows, tokens), BF16),
            pltpu.VMEM((lat_rows, tokens), jnp.int32),
            pltpu.VMEM((lat_count, lat_rows, rows), BF16),
            pltpu.VMEM((2, lat_rows, half), F32),
            pltpu.VMEM((2, layer_count, lat_rows, half), BF16),
            pltpu.VMEM((layer_count, tokens, lat_rows), BF16),
            pltpu.VMEM((lat_count, layer_count, lat_rows, rows), BF16),
            pltpu.VMEM((tokens, rows), F32),
            pltpu.VMEM((tokens, 128), F32),
        ]
        + [slots] * 4
        + [
            pltpu.VMEM((2, half // 2, rows), BF16),
            pltpu.VMEM((tokens, rows), F32),
            pltpu.VMEM((half, rows), F32),
            pltpu.VMEM((lat_count, tokens, rows), BF16),
            pltpu.VMEM((rows, tokens), BF16),
            pltpu.VMEM((layer_count, lat_rows, tokens), F32),
            pltpu.VMEM((pairs, lat_rows, tokens), BF16),
            pltpu.VMEM((pairs, lat_rows, tokens), BF16),
            pltpu.VMEM((pairs - 1, lat_rows, tokens), BF16),
            pltpu.VMEM((layer_count, 8, 128), F32),
            pltpu.VMEM((8, 128), F32),
            pltpu.VMEM((2, lat_count, 8, 128), F32),
            dma((2, 2, 2, 4, depth + 1)),
            dma((2, 2)),
            dma((4, 2, 4, depth + 1)),
            dma((2, 2)),
            dma((2, 4, 2, depth)),
            dma((2, 4, 2, depth)),
            dma((2, 2)),
            dma((2, 2, 2, pairs)),
            dma((2, pairs)),
            dma((2, layer_count)),
            dma((2, 2, lat_count)),
            dma((lat_count,)),
            dma((lat_count,)),
            dma((4,)),
            dma((5,)),
        ],
        compiler_params=pltpu.CompilerParams(
            collective_id=2, has_side_effects=True, vmem_limit_bytes=60 << 20
        ),
    )(inputs_local, wanted, enc_weight, enc_bias, gate, dec_weight, dec_bias, ids)


def dec_grad_kernel(acts_ref, grads_ref, out, acts, grads, ring, in_sems, out_sems):
    layer = lax.axis_index("layer")
    slots, block, _ = ring.shape
    _, layer_count, lat_rows, _ = acts.shape
    lat_count, _, rows = grads.shape
    parts = lat_rows // block
    count = layer_count * parts
    fetch_acts = pltpu.make_async_copy(acts_ref, acts, in_sems.at[0])
    fetch_grads = pltpu.make_async_copy(grads_ref, grads, in_sems.at[1])
    fetch_acts.start()
    fetch_grads.start()
    fetch_acts.wait()
    fetch_grads.wait()

    def write(i):
        here = pl.ds(lax.rem(i, parts) * block, block)
        slot = lax.rem(i, slots)
        return pltpu.make_async_copy(
            ring.at[slot], out.at[lax.div(i, parts), here], out_sems.at[slot]
        )

    @pl.loop(0, count)
    def _(i):
        pl.when(i >= slots)(lambda: write(i - slots).wait())
        source, slot = lax.div(i, parts), lax.rem(i, slots)

        @pl.when(source <= layer)
        def _():
            here = pl.ds(lax.rem(i, parts) * block, block)
            left = jnp.concatenate([acts[0, source, here], acts[1, source, here]], axis=1)
            for g in range(lat_count):
                made = jnp.dot(left, grads[g], preferred_element_type=F32)
                ring[slot, :, g * rows : (g + 1) * rows] = made.astype(BF16)

        @pl.when(source > layer)
        def _():
            ring[slot] = jnp.zeros(ring.shape[1:], BF16)

        write(i).start()

    for i in range(max(count - slots, 0), count):
        write(i).wait()


def dec_grad(acts, grads):
    _, layer_count, lat_rows, half = acts.shape
    lat_count, tokens, rows = grads.shape
    features = lat_count * rows
    block = lat_rows // 2
    return pl.pallas_call(
        dec_grad_kernel,
        out_shape=jax.ShapeDtypeStruct((layer_count, lat_rows, features), BF16),
        in_specs=[HBM, HBM],
        out_specs=HBM,
        scratch_shapes=[
            pltpu.VMEM(acts.shape, BF16),
            pltpu.VMEM(grads.shape, BF16),
            pltpu.VMEM((3, block, features), BF16),
            pltpu.SemaphoreType.DMA((2,)),
            pltpu.SemaphoreType.DMA((3,)),
        ],
        cost_estimate=pl.CostEstimate(
            flops=2 * layer_count * lat_rows * tokens * features,
            bytes_accessed=2 * layer_count * lat_rows * features,
            transcendentals=0,
        ),
        compiler_params=pltpu.CompilerParams(vmem_limit_bytes=32 << 20),
    )(acts, grads)


def enc_grad_kernel(term, came, gate, inputs, out):
    total = term[...]
    for k in range(came.shape[0]):
        total = total + came[k].astype(F32)
    left = (gate[...].astype(F32) * total).astype(BF16)
    lat_count, _, rows = inputs.shape
    for g in range(lat_count):
        made = jnp.dot(left, inputs[g], preferred_element_type=F32)
        out[:, g * rows : (g + 1) * rows] = made.astype(BF16)


def enc_grad(term, came, gate, inputs):
    lat_rows, tokens = term.shape
    lat_count, _, rows = inputs.shape
    block = lat_rows // 4
    return pl.pallas_call(
        enc_grad_kernel,
        grid=(4,),
        out_shape=jax.ShapeDtypeStruct((lat_rows, lat_count * rows), BF16),
        in_specs=[
            pl.BlockSpec((block, tokens), lambda r: (r, 0)),
            pl.BlockSpec((came.shape[0], block, tokens), lambda r: (0, r, 0)),
            pl.BlockSpec((block, tokens), lambda r: (r, 0)),
            pl.BlockSpec(inputs.shape, lambda r: (0, 0, 0)),
        ],
        out_specs=pl.BlockSpec((block, lat_count * rows), lambda r: (r, 0)),
        compiler_params=pltpu.CompilerParams(vmem_limit_bytes=32 << 20),
    )(term, came, gate, inputs)


def gather_inputs(inputs_local, wanted, lat_count):
    rows, tokens = inputs_local.shape
    depth = lat_count // 2
    return pl.pallas_call(
        functools.partial(gather_kernel, lat_count),
        out_shape=(
            jax.ShapeDtypeStruct((lat_count, rows, tokens), BF16),
            jax.ShapeDtypeStruct((lat_count, 8, 128), F32),
        ),
        in_specs=[VMEM] * 2,
        out_specs=(VMEM, VMEM),
        scratch_shapes=[
            pltpu.VMEM((8, 128), F32),
            pltpu.SemaphoreType.DMA((2, 4, depth + 1)),
            pltpu.SemaphoreType.DMA((2, 4, depth + 1)),
            pltpu.SemaphoreType.DMA,
        ],
        compiler_params=pltpu.CompilerParams(
            collective_id=0, has_side_effects=True, vmem_limit_bytes=32 << 20
        ),
    )(inputs_local, wanted)


def reduce_and_gather(parts, wanted, bias, kept, spread, lat_count):
    _, rows, tokens = parts.shape
    depth = lat_count // 2
    slots = pltpu.VMEM((depth, rows, tokens), BF16)
    return pl.pallas_call(
        functools.partial(reduce_kernel, lat_count),
        out_shape=(
            jax.ShapeDtypeStruct((lat_count, rows, tokens), BF16),
            jax.ShapeDtypeStruct((lat_count, 8, 128), F32),
        ),
        in_specs=[VMEM] * 5,
        out_specs=(VMEM, VMEM),
        scratch_shapes=[slots] * 6
        + [
            pltpu.VMEM((rows, tokens), F32),
            pltpu.VMEM((rows, tokens), BF16),
            pltpu.VMEM((8, 128), F32),
            pltpu.SemaphoreType.DMA((2, 2, depth)),
            pltpu.SemaphoreType.DMA((2, 2, depth)),
            pltpu.SemaphoreType.DMA((2, 4, depth + 1)),
            pltpu.SemaphoreType.DMA((2, 4, depth + 1)),
        ],
        compiler_params=pltpu.CompilerParams(
            collective_id=1, has_side_effects=True, vmem_limit_bytes=40 << 20
        ),
    )(parts, wanted, bias, kept, spread)


def on_device(
    resid_in, resid_out, token_ids, active_mask, enc_weight, enc_bias, dec_weight, dec_bias
):
    layer_count = lax.axis_size("layer")
    lat_count = lax.axis_size("lat")
    lat_rows = enc_weight.shape[1]
    feature_rows, token_count = resid_in.shape[1:]
    fused = feature_rows % 128 == 0 and lat_rows % 128 == 0 and token_count == 256
    fused = fused and layer_count % 2 == 0 and layer_count > 2 and lat_count == 8
    args = (
        resid_in, resid_out, token_ids, active_mask, enc_weight, enc_bias, dec_weight, dec_bias
    )
    return fused_step(*args) if fused else plain_step(*args)


def fused_step(
    resid_in, resid_out, token_ids, active_mask, enc_weight, enc_bias, dec_weight, dec_bias
):
    layer_count = lax.axis_size("layer")
    pairs = layer_count // 2
    inputs, grads, acts, own_term, terms, loss_tile = step(
        resid_in[0],
        resid_out[0],
        enc_weight[0],
        enc_bias,
        active_mask[0],
        dec_weight[0],
        dec_bias,
        token_ids[None, :],
        lax.axis_size("lat"),
    )
    came = [
        lax.ppermute(
            terms[k - 1], "layer", [(d, d - 2 * k) for d in range(2 * k, layer_count)]
        )[None]
        for k in range(1, pairs)
    ]
    came = came[0] if pairs == 2 else jnp.concatenate(came, axis=0)
    dec_out = dec_grad(acts, grads)
    enc_out = enc_grad(own_term, came, active_mask[0], inputs)
    return (enc_out[None], dec_out[None], loss_tile.reshape(()))


def plain_step(
    resid_in, resid_out, token_ids, active_mask, enc_weight, enc_bias, dec_weight, dec_bias
):
    layer_count = lax.axis_size("layer")
    lat_count = lax.axis_size("lat")
    layer_here = lax.axis_index("layer")
    inputs_local = resid_in[0]
    wanted = resid_out[0]
    weight_enc = enc_weight[0]
    lat_rows = weight_enc.shape[0]
    feature_count = weight_enc.shape[1]
    feature_rows, token_count = inputs_local.shape
    total_cells = feature_count * token_count
    kept_tokens = (token_ids != 128000).astype(F32)
    source_ids = jnp.arange(layer_count)
    gating = active_mask[0].astype(F32)
    weight_rows = dec_weight[0].reshape(layer_count * lat_rows, feature_count)
    whole_inputs, target_stats = gather_inputs(inputs_local, wanted, lat_count)
    whole_inputs = whole_inputs.reshape(feature_count, token_count)
    spread = jnp.sum(target_stats[:, 0, 0]) / total_cells + EPSILON
    preact = jnp.dot(weight_enc, whole_inputs, preferred_element_type=F32)
    preact = preact + enc_bias[0].astype(F32)[:, None]
    latents = (gating * preact).astype(BF16)
    gathered = lax.all_gather(latents[None], "layer", axis=0, tiled=True)
    acts_stack = jnp.where(
        (source_ids <= layer_here)[:, None, None], gathered, jnp.zeros((), BF16)
    )
    stack_rows = acts_stack.reshape(layer_count * lat_rows, token_count)
    parts = lax.dot_general(
        weight_rows, stack_rows, (((0,), (0,)), ((), ())), preferred_element_type=F32
    ).astype(BF16)
    full_grad, err_stats = reduce_and_gather(
        parts.reshape(lat_count, feature_rows, token_count),
        wanted,
        dec_bias[0].astype(F32)[:, None],
        kept_tokens[None, :],
        jnp.broadcast_to(spread, (1, token_count)),
        lat_count,
    )
    full_grad = full_grad.reshape(feature_count, token_count)
    layer_loss = jnp.sum(err_stats[:, 0, 0]) / (2.0 * spread * total_cells)
    total_loss = lax.psum(layer_loss, "layer")
    grad_rows = jnp.dot(weight_rows, full_grad, preferred_element_type=F32).reshape(
        layer_count, lat_rows, token_count
    )
    grad_rows = (grad_rows * (source_ids <= layer_here).astype(F32)[:, None, None]).astype(BF16)
    dec_out = lax.dot_general(
        stack_rows, full_grad, (((1,), (1,)), ((), ())), preferred_element_type=F32
    )
    dec_out = dec_out.astype(BF16).reshape(1, layer_count, lat_rows, feature_count)
    latent_grad = lax.psum_scatter(grad_rows, "layer", scatter_dimension=0, tiled=True)[0]
    preact_grad = (gating * latent_grad.astype(F32)).astype(BF16)
    enc_out = lax.dot_general(
        preact_grad, whole_inputs, (((1,), (1,)), ((), ())), preferred_element_type=F32
    )
    return (enc_out.astype(BF16)[None], dec_out, total_loss)


def solution(mesh):
    in_specs = (
        P("layer", "lat", None),
        P("layer", "lat", None),
        P(),
        P("layer", "lat", None),
        P("layer", "lat", None),
        P("layer", "lat"),
        P("layer", None, "lat", None),
        P("layer", "lat"),
    )
    out_specs = (P("layer", "lat", None), P("layer", None, "lat", None), P())
    return jax.shard_map(
        on_device, mesh=mesh, in_specs=in_specs, out_specs=out_specs, check_vma=False
    )
```

```python
import functools

import jax
import jax.numpy as jnp
from jax import lax
from jax.experimental import pallas as pl
from jax.experimental.pallas import tpu as pltpu
from jax.sharding import PartitionSpec as P

EPSILON = 1e-05
F32 = jnp.float32
BF16 = jnp.bfloat16


class Place:
    def __init__(self, lat_count):
        self.me = lax.axis_index("lat")
        self.depth = lat_count // 2
        self.z = self.me // 2
        self.y = self.me % 2
        self.partner = self.me + 1 - 2 * self.y
        self.has_up = self.z < self.depth - 1
        self.has_down = self.z > 0


def send(src, dst, send_sem, recv_sem, lat):
    return pltpu.make_async_remote_copy(
        src_ref=src,
        dst_ref=dst,
        send_sem=send_sem,
        recv_sem=recv_sem,
        device_id={"lat": lat},
        device_id_type=pl.DeviceIdType.MESH,
    )


def greet(at, more=0):
    barrier = pltpu.get_barrier_semaphore()

    def hello(lat):
        pl.semaphore_signal(
            barrier, inc=1, device_id={"lat": lat}, device_id_type=pl.DeviceIdType.MESH
        )

    hello(at.partner)
    pl.when(at.has_up)(lambda: hello(at.me + 2))
    pl.when(at.has_down)(lambda: hello(at.me - 2))
    peers = 1 + more + at.has_up.astype(jnp.int32) + at.has_down.astype(jnp.int32)
    pl.semaphore_wait(barrier, peers)


class Gather:
    def __init__(self, at, own, whole, sems):
        self.at, self.own, self.whole, self.sems = at, own, whole, sems

    def hop(self, kind, d):
        at = self.at
        shard = at.me - 2 * d if kind in (0, 2) else at.me + 2 * d
        src = self.own if d == 0 else self.whole.at[shard]
        to = (at.me + 2, at.me - 2, at.partner, at.partner)[kind]
        later = d + 1 if kind < 2 else d
        return send(
            src, self.whole.at[shard], self.sems.at[0, kind, d], self.sems.at[1, kind, later], to
        )

    def landing(self, kind, d):
        at = self.at
        below = kind in (0, 2)
        shard = at.me - 2 * d if below else at.me + 2 * d
        if kind >= 2:
            shard = shard + 1 - 2 * at.y
        ref = self.whole.at[shard]
        return send(ref, ref, self.sems.at[0, kind, d], self.sems.at[1, kind, d], at.partner)

    def start(self):
        pl.when(self.at.has_up)(lambda: self.hop(0, 0).start())
        pl.when(self.at.has_down)(lambda: self.hop(1, 0).start())
        self.hop(2, 0).start()

    def step(self, d):
        at = self.at

        @pl.when(at.z >= d)
        def _():
            self.landing(0, d).wait_recv()
            pl.when(at.has_up)(lambda: self.hop(0, d).start())
            self.hop(2, d).start()

        @pl.when(at.z + d < at.depth)
        def _():
            self.landing(1, d).wait_recv()
            pl.when(at.has_down)(lambda: self.hop(1, d).start())
            self.hop(3, d).start()

    def finish(self, crossed=False):
        at = self.at
        for d in range(at.depth):

            @pl.when(at.z >= d)
            def _():
                if not crossed:
                    self.landing(2, d).wait_recv()
                self.hop(2, d).wait_send()
                if d < at.depth - 1:
                    pl.when(at.has_up)(lambda: self.hop(0, d).wait_send())

            @pl.when(at.z + d < at.depth)
            def _():
                if d > 0:
                    if not crossed:
                        self.landing(3, d).wait_recv()
                    self.hop(3, d).wait_send()
                if d < at.depth - 1:
                    pl.when(at.has_down)(lambda: self.hop(1, d).wait_send())


def gather_kernel(lat_count, own, wanted_ref, whole, stats, stat, big_sems, stat_sems, local_sem):
    at = Place(lat_count)
    greet(at)
    big = Gather(at, own, whole, big_sems)
    big.start()
    keep = pltpu.make_async_copy(own, whole.at[at.me], local_sem)
    keep.start()
    wanted = wanted_ref[...].astype(F32)
    centered = wanted - jnp.mean(wanted, axis=1, keepdims=True)
    total = jnp.sum(centered * centered, keepdims=True)
    stat[...] = jnp.broadcast_to(total, stat.shape)
    stats[at.me] = stat[...]
    small = Gather(at, stat, stats, stat_sems)
    small.start()
    for d in range(1, at.depth):
        big.step(d)
        small.step(d)
    keep.wait()
    big.finish()
    small.finish()


def reduce_kernel(
    lat_count,
    parts,
    wanted_ref,
    bias_ref,
    kept_ref,
    spread_ref,
    whole,
    stats,
    across_up,
    across_down,
    from_below,
    from_above,
    going_up,
    going_down,
    total,
    grad,
    stat,
    across_sems,
    line_sems,
    big_sems,
    stat_sems,
):
    at = Place(lat_count)
    depth = at.depth
    greet(at)

    def across(up, d):
        rung = at.z + d if up else at.z - d
        row = 0 if up else 1
        return send(
            parts.at[rung * 2 + 1 - at.y],
            (across_up if up else across_down).at[d],
            across_sems.at[0, row, d],
            across_sems.at[1, row, d],
            at.partner,
        )

    def along(up, d):
        row = 0 if up else 1
        return send(
            (going_up if up else going_down).at[d],
            (from_below if up else from_above).at[d - 1],
            line_sems.at[0, row, d],
            line_sems.at[1, row, d - 1],
            at.me + 2 if up else at.me - 2,
        )

    def arrived(up, d):
        row = 0 if up else 1
        ref = (from_below if up else from_above).at[d]
        send(ref, ref, line_sems.at[0, row, d], line_sems.at[1, row, d], at.partner).wait_recv()

    for d in range(depth - 1, -1, -1):
        pl.when(at.z + d < depth)(lambda: across(True, d).start())
        if d:
            pl.when(at.z >= d)(lambda: across(False, d).start())

    def forward(up, d):
        across(up, d).wait_recv()
        rung = at.z + d if up else at.z - d
        crossed = across_up if up else across_down
        came = from_below if up else from_above
        going = going_up if up else going_down
        behind = at.has_down if up else at.has_up
        mine = parts.at[rung * 2 + at.y]

        @pl.when(behind)
        def _():
            if d < depth - 1:
                arrived(up, d)
                going[d] = (
                    mine[...].astype(F32) + crossed[d].astype(F32) + came[d].astype(F32)
                ).astype(BF16)

        @pl.when(jnp.logical_not(behind))
        def _():
            going[d] = (mine[...].astype(F32) + crossed[d].astype(F32)).astype(BF16)

        along(up, d).start()

    for d in range(depth - 1, 0, -1):
        pl.when(at.z + d < depth)(lambda: forward(True, d))
        pl.when(at.z >= d)(lambda: forward(False, d))
    across(True, 0).wait_recv()
    total[...] = (
        parts[at.me].astype(F32)
        + across_up[0].astype(F32)
        + (bias_ref[...] - wanted_ref[...].astype(F32))
    )

    @pl.when(at.has_down)
    def _():
        arrived(True, 0)
        total[...] += from_below[0].astype(F32)

    @pl.when(at.has_up)
    def _():
        arrived(False, 0)
        total[...] += from_above[0].astype(F32)

    err = kept_ref[...] * total[...]
    grad[...] = (err / spread_ref[...]).astype(BF16)
    whole[at.me] = grad[...]
    big = Gather(at, grad, whole, big_sems)
    big.start()
    stat[...] = jnp.broadcast_to(jnp.sum(err * err, keepdims=True), stat.shape)
    stats[at.me] = stat[...]
    small = Gather(at, stat, stats, stat_sems)
    small.start()
    for d in range(1, depth):
        big.step(d)
        small.step(d)
    big.finish()
    small.finish()
    for d in range(depth - 1, -1, -1):

        @pl.when(at.z + d < depth)
        def _():
            across(True, d).wait_send()
            if d:
                along(True, d).wait_send()

        if d:

            @pl.when(at.z >= d)
            def _():
                across(False, d).wait_send()
                along(False, d).wait_send()


def to_layer(src, dst, send_sem, recv_sem, layer):
    return pltpu.make_async_remote_copy(
        src_ref=src,
        dst_ref=dst,
        send_sem=send_sem,
        recv_sem=recv_sem,
        device_id={"layer": layer},
        device_id_type=pl.DeviceIdType.MESH,
    )


class Spread:
    def __init__(self, at, ref, sems, pair_sems):
        self.at, self.ref, self.sems, self.pair_sems = at, ref, sems, pair_sems

    def shard_of(self, kind, d, landing=False):
        at = self.at
        shard = at.me - 2 * d if kind in (0, 2) else at.me + 2 * d
        if landing and kind >= 2:
            shard = shard + 1 - 2 * at.y
        return shard

    def hop(self, kind, d):
        at = self.at
        ref = self.ref(self.shard_of(kind, d))
        later = d + 1 if kind < 2 else d
        to = (at.me + 2, at.me - 2, at.partner, at.partner)[kind]
        return send(ref, ref, self.sems.at[0, kind, d], self.sems.at[1, kind, later], to)

    def landing(self, kind, d):
        ref = self.ref(self.shard_of(kind, d, True))
        return send(
            ref, ref, self.sems.at[0, kind, d], self.sems.at[1, kind, d], self.at.partner
        )

    def crossing(self, what, kind, d, act):
        if d != 1 or self.pair_sems is None:
            act(what(kind, d))
            return
        straight = jnp.logical_not(self.at.odd) if kind == 2 else self.at.odd
        pl.when(straight)(lambda: act(what(kind, d)))

    def aside(self, landing=False):
        at = self.at
        ref = self.ref(at.beside + 1 - 2 * at.y if landing else at.partner)
        return send(ref, ref, self.pair_sems.at[0], self.pair_sems.at[1], at.beside)

    def start(self):
        self.hop(2, 0).start()
        pl.when(self.at.has_up)(lambda: self.hop(0, 0).start())
        pl.when(self.at.has_down)(lambda: self.hop(1, 0).start())

    def line(self, d):
        at = self.at

        @pl.when(at.z >= d)
        def _():
            self.landing(0, d).wait_recv()
            pl.when(at.has_up)(lambda: self.hop(0, d).start())
            self.crossing(self.hop, 2, d, lambda one: one.start())

        @pl.when(at.z + d < at.depth)
        def _():
            self.landing(1, d).wait_recv()
            pl.when(at.has_down)(lambda: self.hop(1, d).start())
            self.crossing(self.hop, 3, d, lambda one: one.start())

    def settle(self, d):
        at = self.at
        if d == 0:
            self.landing(2, 0).wait_recv()
            if self.pair_sems is not None:
                self.aside().start()
            return
        if d == 1 and self.pair_sems is not None:
            self.aside(True).wait_recv()
        arrive = lambda one: one.wait_recv()
        pl.when(at.z >= d)(lambda: self.crossing(self.landing, 2, d, arrive))
        pl.when(at.z + d < at.depth)(lambda: self.crossing(self.landing, 3, d, arrive))

    def finish(self):
        at = self.at
        if self.pair_sems is not None:
            self.aside().wait_send()
        for d in range(at.depth):

            @pl.when(at.z >= d)
            def _():
                self.crossing(self.hop, 2, d, lambda one: one.wait_send())
                if d < at.depth - 1:
                    pl.when(at.has_up)(lambda: self.hop(0, d).wait_send())

            @pl.when(at.z + d < at.depth)
            def _():
                if d > 0:
                    self.crossing(self.hop, 3, d, lambda one: one.wait_send())
                if d < at.depth - 1:
                    pl.when(at.has_down)(lambda: self.hop(1, d).wait_send())


def advance(at, *stages):
    for group, d, use in stages:
        if 0 < d < at.depth:
            for one in group:
                one.line(d)
    for group, d, use in stages:
        if d == 0:
            for one in group:
                one.start()
    for group, d, use in stages:
        if d == 1:
            use(at.me)
        if 0 < d < at.depth:
            pl.when(at.z >= d)(lambda: use(at.me - 2 * d))
            pl.when(at.z + d < at.depth)(lambda: use(at.me + 2 * d))
    for group, d, use in stages:
        if d > 0:
            for one in group:
                one.settle(d - 1)
    for group, d, use in stages:
        if d > 0:
            pl.when(at.z >= d - 1)(lambda: use(at.partner - 2 * (d - 1)))
        if d > 1:
            pl.when(at.z + d - 1 < at.depth)(lambda: use(at.partner + 2 * (d - 1)))


def step_kernel(
    lat_count,
    own,
    wanted_ref,
    enc_weight,
    enc_bias,
    gate_ref,
    dec_weight,
    dec_bias,
    ids_ref,
    turned_x_out,
    grads_out,
    acts_out,
    own_term_out,
    terms_out,
    loss,
    whole_x,
    turned_x,
    wanted_here,
    gate_here,
    enc_blocks,
    acc_enc,
    acts,
    turned,
    blocks,
    base,
    kept,
    leaving,
    crossed,
    came,
    going,
    pair_in,
    fresh,
    whole_g,
    column,
    acc,
    giving,
    given,
    terms,
    losses,
    spread_tile,
    stats,
    x_sems,
    x_pair_sems,
    g_sems,
    g_pair_sems,
    across_sems,
    line_sems,
    pair_sems,
    layer_sems,
    mate_sems,
    loss_sems,
    stat_sems,
    enc_sems,
    block_sems,
    local_sems,
    out_sems,
):
    at = Place(lat_count)
    at.odd = at.z % 2 == 1
    at.beside = at.me + 2 - 4 * (at.z % 2)
    depth = at.depth
    layer_count = acts.shape[1]
    rows, half = whole_x.shape[2:]
    piece = half // 2
    layer = lax.axis_index("layer")
    pairs = layer_count // 2
    pair, core = layer // 2, layer % 2
    mate = layer + 1 - 2 * core
    cells = lat_count * rows * half * 2

    def own_half(h):
        return pltpu.make_async_copy(
            own.at[:, pl.ds(h * half, half)], whole_x.at[h, at.me], local_sems.at[h]
        )

    def load_enc(g):
        return pltpu.make_async_copy(
            enc_weight.at[:, pl.ds(g * rows, rows)], enc_blocks.at[g], enc_sems.at[g]
        )

    def load_dec(g):
        return pltpu.make_async_copy(
            dec_weight.at[:, :, pl.ds(g * rows, rows)], blocks.at[g], block_sems.at[g]
        )

    fetch = pltpu.make_async_copy(wanted_ref, wanted_here, local_sems.at[2])
    fetch_gate = pltpu.make_async_copy(gate_ref, gate_here, local_sems.at[3])
    own_half(0).start()
    own_half(1).start()
    for g in range(lat_count):
        load_enc(g).start()
    fetch.start()
    fetch_gate.start()

    barrier = pltpu.get_barrier_semaphore()
    for k in range(1, layer_count):
        other = lax.rem(layer + k, layer_count)
        pl.semaphore_signal(
            barrier, inc=1, device_id={"layer": other}, device_id_type=pl.DeviceIdType.MESH
        )
    own_half(0).wait()
    own_half(1).wait()
    greet(at, layer_count - 1)

    def tally(which):
        return Spread(at, lambda shard: stats.at[which, shard], stat_sems.at[which], None)

    def feature_piece(h, q):
        def ref(shard):
            return whole_x.at[h, shard, pl.ds(q * (rows // 2), rows // 2)]

        return Spread(at, ref, x_sems.at[h, q], x_pair_sems.at[h] if q else None)

    def use_x(h):
        def use(g):
            acc_enc[h] += jnp.dot(enc_blocks[g], whole_x[h, g], preferred_element_type=F32)

        return use

    gather_x = [[feature_piece(h, q) for q in range(2)] for h in range(2)]
    gather_x.append([tally(0)])

    def stage_x(*which):
        uses = use_x(0), use_x(1), lambda g: None
        advance(at, *[(gather_x[h], d, uses[h]) for h, d in which])

    stage_x((0, 0))
    bias = jnp.transpose(jnp.broadcast_to(enc_bias[...].astype(F32), (half, enc_bias.shape[1])))
    acc_enc[0] = bias
    acc_enc[1] = bias
    turned[...] = jnp.zeros_like(turned)
    for g in range(lat_count):
        load_enc(g).wait()
    for g in range(lat_count):
        load_dec(g).start()
    stage_x((0, 1), (1, 0))
    fetch.wait()
    wanted = wanted_here[...].astype(F32)
    centered = wanted - jnp.mean(wanted, axis=1, keepdims=True)
    total = jnp.sum(centered * centered, keepdims=True)
    stats[0, at.me] = jnp.broadcast_to(total, stats.shape[2:])
    stage_x((0, 2), (1, 1), (2, 0))
    stage_x((0, 3), (1, 2), (2, 1))
    base[...] = dec_bias[...].astype(F32) - jnp.transpose(wanted_here[...].astype(F32))
    fetch_gate.wait()
    stage_x((0, 4), (2, 2))

    def over(h, k):
        ref = acts.at[h, layer]
        return to_layer(
            ref, ref, layer_sems.at[0, h, 0, k], layer_sems.at[1, h, 0, k], layer + 2 * k
        )

    def pass_on(h, k):
        ref = acts.at[h, layer - 2 * k]
        return to_layer(ref, ref, layer_sems.at[0, h, 1, k], layer_sems.at[1, h, 1, k], mate)

    def landed(h, kind, k):
        ref = acts.at[h, layer - 2 * k if kind == 0 else mate - 2 * k]
        sem = layer_sems.at[1, h, kind, k]
        return to_layer(ref, ref, layer_sems.at[0, h, kind, k], sem, mate)

    def turn(h, source):
        turned[source, h * half : (h + 1) * half] = jnp.transpose(acts[h, source])

    def exchange(h):
        gate = gate_here[:, h * half : (h + 1) * half].astype(F32)
        acts[h, layer] = (gate * acc_enc[h]).astype(BF16)
        for k in range(1, pairs):
            pl.when(pair + k < pairs)(lambda: over(h, k).start())
        pl.when(core == 0)(lambda: pass_on(h, 0).start())
        turn(h, layer)
        yield
        for k in range(1, pairs):

            @pl.when(pair >= k)
            def _():
                landed(h, 0, k).wait_recv()
                pass_on(h, k).start()
                turn(h, layer - 2 * k)

        yield

        @pl.when(core == 1)
        def _():
            landed(h, 1, 0).wait_recv()
            turn(h, mate)

        for k in range(1, pairs):

            @pl.when(pair >= k)
            def _():
                landed(h, 1, k).wait_recv()
                turn(h, mate - 2 * k)

        yield

    def exchange_sent(h):
        pl.when(core == 0)(lambda: pass_on(h, 0).wait_send())
        for k in range(1, pairs):
            pl.when(pair >= k)(lambda: pass_on(h, k).wait_send())
            pl.when(pair + k < pairs)(lambda: over(h, k).wait_send())

    moves = [exchange(h) for h in range(2)]
    next(moves[0])
    stage_x((1, 3), (2, 3))
    next(moves[0])
    stage_x((1, 4), (2, 4))
    next(moves[1])
    next(moves[0])
    for g in range(lat_count):
        load_dec(g).wait()
    spread_tile[...] = jnp.sum(stats[0], axis=0) / cells + EPSILON
    spread = jnp.max(spread_tile[...], keepdims=True)

    def part(h, g):
        some = slice(h * half, (h + 1) * half)
        got = jnp.dot(turned[0, some], blocks[g, 0], preferred_element_type=F32)
        for source in range(1, layer_count):
            got += jnp.dot(turned[source, some], blocks[g, source], preferred_element_type=F32)
        fresh[...] = got

    def within(p):
        return pl.ds(p % 2 * piece, piece)

    def of(p):
        return pl.ds(p * piece, piece)

    def across(p, up, d):
        row = 0 if up else 1
        return send(
            leaving.at[row, d, of(p)],
            crossed.at[row, d, of(p)],
            across_sems.at[0, p, row, d],
            across_sems.at[1, p, row, d],
            at.partner,
        )

    def aside(p, up):
        return send(
            leaving.at[0 if up else 1, 1, of(p)],
            pair_in.at[p // 2],
            pair_sems.at[0, p // 2],
            pair_sems.at[1, p // 2],
            at.beside,
        )

    def by_side(p, up, d, cross, turn_aside=None):
        if d != 1 or p % 2 == 0:
            cross()
            return
        beside = jnp.logical_not(at.odd) if up else at.odd
        pl.when(jnp.logical_not(beside))(cross)
        if turn_aside is not None:
            pl.when(beside)(turn_aside)

    def along(p, up, d):
        row = 0 if up else 1
        return send(
            going.at[row, d, of(p)],
            came.at[row, d - 1, of(p)],
            line_sems.at[0, p, row, d],
            line_sems.at[1, p, row, d - 1],
            at.me + 2 if up else at.me - 2,
        )

    def arrived(p, up, d):
        row = 0 if up else 1
        ref = came.at[row, d, of(p)]
        sems = line_sems.at[0, p, row, d], line_sems.at[1, p, row, d]
        send(ref, ref, *sems, at.partner).wait_recv()
        fresh[within(p), :] += came[row, d, of(p)].astype(F32)

    def met(p, up, d):
        across(p, up, d).wait_recv()
        fresh[within(p), :] += crossed[0 if up else 1, d, of(p)].astype(F32)

    def leave(h, up, d):
        row = 0 if up else 1
        part(h, at.partner + 2 * d if up else at.partner - 2 * d)
        if d == 0:
            aside(2 * h + 1, True).wait_recv()
            fresh[piece:] += pair_in[h].astype(F32)
        leaving[row, d, h * half : (h + 1) * half] = fresh[...].astype(BF16)
        for p in (2 * h, 2 * h + 1):
            by_side(
                p, up, d, lambda: across(p, up, d).start(), lambda: aside(p, up).start()
            )

    def leaves(h, d):
        pl.when(at.z + d < depth)(lambda: leave(h, True, d))
        if d:
            pl.when(at.z >= d)(lambda: leave(h, False, d))

    def forward(h, up, d):
        row = 0 if up else 1
        part(h, at.me + 2 * d if up else at.me - 2 * d)
        for p in (2 * h, 2 * h + 1):
            by_side(p, up, d, lambda: met(p, up, d))
            if d < depth - 1:
                pl.when(at.has_down if up else at.has_up)(lambda: arrived(p, up, d))
            going[row, d, of(p)] = fresh[within(p), :].astype(BF16)
            along(p, up, d).start()

    def forwards(h, d):
        pl.when(at.z + d < depth)(lambda: forward(h, True, d))
        pl.when(at.z >= d)(lambda: forward(h, False, d))

    def token_piece(p):
        def ref(shard):
            return whole_g.at[shard, of(p)]

        return Spread(at, ref, g_sems.at[p], g_pair_sems.at[p // 2] if p % 2 else None)

    gather_g = [token_piece(p) for p in range(4)]
    gather_g.append(tally(1))

    def use_g(g):
        column[...] = jnp.transpose(whole_g[g])
        for source in range(layer_count):
            acc[source] += jnp.dot(blocks[g, source], column[...], preferred_element_type=F32)

    def close(h):
        part(h, at.me)
        fresh[...] += base[h * half : (h + 1) * half]
        for p in (2 * h, 2 * h + 1):
            met(p, True, 0)
            pl.when(at.has_down)(lambda: arrived(p, True, 0))
            pl.when(at.has_up)(lambda: arrived(p, False, 0))
            err = kept[of(p), :1] * fresh[within(p), :]
            whole_g[at.me, of(p)] = (err / spread).astype(BF16)
            gather_g[p].start()
            total = jnp.sum(err * err, keepdims=True)
            if p == 0:
                stats[1, at.me] = jnp.broadcast_to(total, stats.shape[2:])
            else:
                stats[1, at.me] += total
        if h:
            gather_g[4].start()

    def turn_x(g):
        for h in range(2):
            turned_x[g, h * half : (h + 1) * half] = jnp.transpose(whole_x[h, g])

    def stage_g(*which):
        uses = turn_x, use_g
        advance(at, *[(gather_g[2 * h : 2 * h + 2 + h], d, uses[h]) for h, d in which])

    leaves(0, 3)
    leaves(0, 2)
    leaves(0, 1)
    next(moves[1])
    forwards(0, 3)
    next(moves[1])
    leaves(1, 3)
    forwards(0, 2)
    leaves(1, 2)
    leaves(0, 0)
    forwards(0, 1)
    leaves(1, 1)
    forwards(1, 3)
    ids = jnp.broadcast_to((ids_ref[...] != 128000).astype(F32), (128, 2 * half))
    kept[...] = jnp.transpose(ids)
    close(0)
    forwards(1, 2)
    leaves(1, 0)
    stage_g((0, 1))
    forwards(1, 1)
    stage_g((0, 2))
    acc[...] = jnp.zeros_like(acc)
    close(1)
    stage_g((0, 3), (1, 1))
    stage_g((0, 4), (1, 2))
    stage_g((1, 3))

    def out(which):
        src, dst = (
            (turned_x, turned_x_out),
            (acts, acts_out),
            (whole_g, grads_out),
            (acc.at[layer], own_term_out),
            (terms, terms_out),
        )[which]
        return pltpu.make_async_copy(src, dst, out_sems.at[which])

    out(0).start()
    out(1).start()
    stage_g((1, 4))
    out(2).start()
    losses[layer] = jnp.sum(stats[1], axis=0) / (2.0 * spread_tile[...] * cells)

    def tell(k, told=False):
        other = lax.rem(layer + (layer_count - k if told else k), layer_count)
        ref = losses.at[other if told else layer]
        return to_layer(ref, ref, loss_sems.at[0, k], loss_sems.at[1, k], other)

    def give(k):
        return to_layer(
            giving.at[k], given.at[k], mate_sems.at[0, k], mate_sems.at[1, k], mate
        )

    def hand(k):
        giving[k] = acc[mate - 2 * k].astype(BF16)
        give(k).start()

    for k in range(pairs - 1, 0, -1):
        pl.when(pair >= k)(lambda: hand(k))
    pl.when(core == 1)(lambda: hand(0))
    for k in range(1, layer_count):
        tell(k).start()
    for k in range(pairs - 1, 0, -1):

        @pl.when(pair >= k)
        def _():
            give(k).wait_recv()
            terms[k - 1] = (acc[layer - 2 * k] + given[k].astype(F32)).astype(BF16)
            give(k).wait_send()

        @pl.when(pair < k)
        def _():
            terms[k - 1] = jnp.zeros(terms.shape[1:], BF16)

    out(4).start()

    @pl.when(core == 0)
    def _():
        give(0).wait_recv()
        acc[layer] += given[0].astype(F32)

    out(3).start()
    pl.when(core == 1)(lambda: give(0).wait_send())
    for k in range(1, layer_count):
        tell(k, True).wait_recv()
        tell(k).wait_send()
    loss[...] = jnp.sum(losses[...], axis=0)[:1, :1]
    for group in gather_x:
        for one in group:
            one.finish()
    for h in range(2):
        exchange_sent(h)
    for one in gather_g:
        one.finish()
    for p in range(4):
        if p % 2:
            aside(p, True).wait_send()
        for d in range(depth):
            for up in (True, False):
                if d or up:

                    @pl.when(at.z + d < depth if up else at.z >= d)
                    def _():
                        by_side(p, up, d, lambda: across(p, up, d).wait_send())
                        if d:
                            along(p, up, d).wait_send()

    for which in range(5):
        out(which).wait()


VMEM = pl.BlockSpec(memory_space=pltpu.VMEM)
HBM = pl.BlockSpec(memory_space=pltpu.HBM)


def step(inputs_local, wanted, enc_weight, enc_bias, gate, dec_weight, dec_bias, ids, lat_count):
    rows, tokens = inputs_local.shape
    layer_count, lat_rows, _ = dec_weight.shape
    depth = lat_count // 2
    pairs = layer_count // 2
    half = tokens // 2
    slots = pltpu.VMEM((2, depth, tokens, rows), BF16)
    dma = pltpu.SemaphoreType.DMA
    return pl.pallas_call(
        functools.partial(step_kernel, lat_count),
        out_shape=(
            jax.ShapeDtypeStruct((lat_count, tokens, rows), BF16),
            jax.ShapeDtypeStruct((lat_count, tokens, rows), BF16),
            jax.ShapeDtypeStruct((2, layer_count, lat_rows, half), BF16),
            jax.ShapeDtypeStruct((lat_rows, tokens), F32),
            jax.ShapeDtypeStruct((pairs - 1, lat_rows, tokens), BF16),
            jax.ShapeDtypeStruct((1, 1), F32),
        ),
        in_specs=[HBM, HBM, HBM, VMEM, HBM, HBM, VMEM, VMEM],
        out_specs=(HBM,) * 5 + (VMEM,),
        scratch_shapes=[
            pltpu.VMEM((2, lat_count, rows, half), BF16),
            pltpu.VMEM((lat_count, tokens, rows), BF16),
            pltpu.VMEM((rows, tokens), BF16),
            pltpu.VMEM((lat_rows, tokens), jnp.int32),
            pltpu.VMEM((lat_count, lat_rows, rows), BF16),
            pltpu.VMEM((2, lat_rows, half), F32),
            pltpu.VMEM((2, layer_count, lat_rows, half), BF16),
            pltpu.VMEM((layer_count, tokens, lat_rows), BF16),
            pltpu.VMEM((lat_count, layer_count, lat_rows, rows), BF16),
            pltpu.VMEM((tokens, rows), F32),
            pltpu.VMEM((tokens, 128), F32),
        ]
        + [slots] * 4
        + [
            pltpu.VMEM((2, half // 2, rows), BF16),
            pltpu.VMEM((half, rows), F32),
            pltpu.VMEM((lat_count, tokens, rows), BF16),
            pltpu.VMEM((rows, tokens), BF16),
            pltpu.VMEM((layer_count, lat_rows, tokens), F32),
            pltpu.VMEM((pairs, lat_rows, tokens), BF16),
            pltpu.VMEM((pairs, lat_rows, tokens), BF16),
            pltpu.VMEM((pairs - 1, lat_rows, tokens), BF16),
            pltpu.VMEM((layer_count, 8, 128), F32),
            pltpu.VMEM((8, 128), F32),
            pltpu.VMEM((2, lat_count, 8, 128), F32),
            dma((2, 2, 2, 4, depth + 1)),
            dma((2, 2)),
            dma((4, 2, 4, depth + 1)),
            dma((2, 2)),
            dma((2, 4, 2, depth)),
            dma((2, 4, 2, depth)),
            dma((2, 2)),
            dma((2, 2, 2, pairs)),
            dma((2, pairs)),
            dma((2, layer_count)),
            dma((2, 2, 4, depth + 1)),
            dma((lat_count,)),
            dma((lat_count,)),
            dma((4,)),
            dma((5,)),
        ],
        compiler_params=pltpu.CompilerParams(
            collective_id=2, has_side_effects=True, vmem_limit_bytes=60 << 20
        ),
    )(inputs_local, wanted, enc_weight, enc_bias, gate, dec_weight, dec_bias, ids)


def dec_grad_kernel(acts_ref, grads_ref, out, acts, grads, ring, in_sems, out_sems):
    layer = lax.axis_index("layer")
    slots, block, _ = ring.shape
    _, layer_count, lat_rows, _ = acts.shape
    lat_count, _, rows = grads.shape
    parts = lat_rows // block
    count = layer_count * parts
    def fetch_acts(source):
        return pltpu.make_async_copy(
            acts_ref.at[:, source], acts.at[:, source], in_sems.at[lat_count + source]
        )

    def fetch_grads(g):
        return pltpu.make_async_copy(grads_ref.at[g], grads.at[g], in_sems.at[g])

    fetch_acts(0).start()
    for g in range(lat_count):
        fetch_grads(g).start()
    for source in range(1, layer_count):
        fetch_acts(source).start()
    fetch_acts(0).wait()

    def write(i):
        here = pl.ds(lax.rem(i, parts) * block, block)
        slot = lax.rem(i, slots)
        return pltpu.make_async_copy(
            ring.at[slot], out.at[lax.div(i, parts), here], out_sems.at[slot]
        )

    def made(i, g):
        source, here = lax.div(i, parts), pl.ds(lax.rem(i, parts) * block, block)
        left = jnp.concatenate([acts[0, source, here], acts[1, source, here]], axis=1)
        return jnp.dot(left, grads[g], preferred_element_type=F32).astype(BF16)

    for g in range(lat_count):
        if g % (lat_count // 2) == 0:
            for later in range(g, g + lat_count // 2):
                fetch_grads(later).wait()
        ring[0, :, g * rows : (g + 1) * rows] = made(0, g)
    write(0).start()
    for source in range(1, layer_count):
        fetch_acts(source).wait()

    @pl.loop(1, count)
    def _(i):
        pl.when(i >= slots)(lambda: write(i - slots).wait())
        source, slot = lax.div(i, parts), lax.rem(i, slots)

        @pl.when(source <= layer)
        def _():
            for g in range(lat_count):
                ring[slot, :, g * rows : (g + 1) * rows] = made(i, g)

        @pl.when(source > layer)
        def _():
            ring[slot] = jnp.zeros(ring.shape[1:], BF16)

        write(i).start()

    for i in range(max(count - slots, 0), count):
        write(i).wait()


def dec_grad(acts, grads):
    _, layer_count, lat_rows, half = acts.shape
    lat_count, tokens, rows = grads.shape
    features = lat_count * rows
    block = lat_rows // 2
    return pl.pallas_call(
        dec_grad_kernel,
        out_shape=jax.ShapeDtypeStruct((layer_count, lat_rows, features), BF16),
        in_specs=[HBM, HBM],
        out_specs=HBM,
        scratch_shapes=[
            pltpu.VMEM(acts.shape, BF16),
            pltpu.VMEM(grads.shape, BF16),
            pltpu.VMEM((3, block, features), BF16),
            pltpu.SemaphoreType.DMA((lat_count + layer_count,)),
            pltpu.SemaphoreType.DMA((3,)),
        ],
        cost_estimate=pl.CostEstimate(
            flops=2 * layer_count * lat_rows * tokens * features,
            bytes_accessed=2 * layer_count * lat_rows * features,
            transcendentals=0,
        ),
        compiler_params=pltpu.CompilerParams(vmem_limit_bytes=60 << 20),
    )(acts, grads)


def enc_grad_kernel(term, came, gate, inputs, out):
    total = term[...]
    for k in range(came.shape[0]):
        total = total + came[k].astype(F32)
    left = (gate[...].astype(F32) * total).astype(BF16)
    lat_count, _, rows = inputs.shape
    for g in range(lat_count):
        made = jnp.dot(left, inputs[g], preferred_element_type=F32)
        out[:, g * rows : (g + 1) * rows] = made.astype(BF16)


def enc_grad(term, came, gate, inputs):
    lat_rows, tokens = term.shape
    lat_count, _, rows = inputs.shape
    block = lat_rows // 4
    return pl.pallas_call(
        enc_grad_kernel,
        grid=(4,),
        out_shape=jax.ShapeDtypeStruct((lat_rows, lat_count * rows), BF16),
        in_specs=[
            pl.BlockSpec((block, tokens), lambda r: (r, 0)),
            pl.BlockSpec((came.shape[0], block, tokens), lambda r: (0, r, 0)),
            pl.BlockSpec((block, tokens), lambda r: (r, 0)),
            pl.BlockSpec(inputs.shape, lambda r: (0, 0, 0)),
        ],
        out_specs=pl.BlockSpec((block, lat_count * rows), lambda r: (r, 0)),
        compiler_params=pltpu.CompilerParams(vmem_limit_bytes=32 << 20),
    )(term, came, gate, inputs)


def gather_inputs(inputs_local, wanted, lat_count):
    rows, tokens = inputs_local.shape
    depth = lat_count // 2
    return pl.pallas_call(
        functools.partial(gather_kernel, lat_count),
        out_shape=(
            jax.ShapeDtypeStruct((lat_count, rows, tokens), BF16),
            jax.ShapeDtypeStruct((lat_count, 8, 128), F32),
        ),
        in_specs=[VMEM] * 2,
        out_specs=(VMEM, VMEM),
        scratch_shapes=[
            pltpu.VMEM((8, 128), F32),
            pltpu.SemaphoreType.DMA((2, 4, depth + 1)),
            pltpu.SemaphoreType.DMA((2, 4, depth + 1)),
            pltpu.SemaphoreType.DMA,
        ],
        compiler_params=pltpu.CompilerParams(
            collective_id=0, has_side_effects=True, vmem_limit_bytes=32 << 20
        ),
    )(inputs_local, wanted)


def reduce_and_gather(parts, wanted, bias, kept, spread, lat_count):
    _, rows, tokens = parts.shape
    depth = lat_count // 2
    slots = pltpu.VMEM((depth, rows, tokens), BF16)
    return pl.pallas_call(
        functools.partial(reduce_kernel, lat_count),
        out_shape=(
            jax.ShapeDtypeStruct((lat_count, rows, tokens), BF16),
            jax.ShapeDtypeStruct((lat_count, 8, 128), F32),
        ),
        in_specs=[VMEM] * 5,
        out_specs=(VMEM, VMEM),
        scratch_shapes=[slots] * 6
        + [
            pltpu.VMEM((rows, tokens), F32),
            pltpu.VMEM((rows, tokens), BF16),
            pltpu.VMEM((8, 128), F32),
            pltpu.SemaphoreType.DMA((2, 2, depth)),
            pltpu.SemaphoreType.DMA((2, 2, depth)),
            pltpu.SemaphoreType.DMA((2, 4, depth + 1)),
            pltpu.SemaphoreType.DMA((2, 4, depth + 1)),
        ],
        compiler_params=pltpu.CompilerParams(
            collective_id=1, has_side_effects=True, vmem_limit_bytes=40 << 20
        ),
    )(parts, wanted, bias, kept, spread)


def on_device(
    resid_in, resid_out, token_ids, active_mask, enc_weight, enc_bias, dec_weight, dec_bias
):
    layer_count = lax.axis_size("layer")
    lat_count = lax.axis_size("lat")
    lat_rows = enc_weight.shape[1]
    feature_rows, token_count = resid_in.shape[1:]
    fused = feature_rows % 128 == 0 and lat_rows % 128 == 0 and token_count == 256
    fused = fused and layer_count % 2 == 0 and layer_count > 2 and lat_count == 8
    args = (
        resid_in, resid_out, token_ids, active_mask, enc_weight, enc_bias, dec_weight, dec_bias
    )
    return fused_step(*args) if fused else plain_step(*args)


def fused_step(
    resid_in, resid_out, token_ids, active_mask, enc_weight, enc_bias, dec_weight, dec_bias
):
    layer_count = lax.axis_size("layer")
    pairs = layer_count // 2
    inputs, grads, acts, own_term, terms, loss_tile = step(
        resid_in[0],
        resid_out[0],
        enc_weight[0],
        enc_bias,
        active_mask[0],
        dec_weight[0],
        dec_bias,
        token_ids[None, :],
        lax.axis_size("lat"),
    )
    came = [
        lax.ppermute(
            terms[k - 1], "layer", [(d, d - 2 * k) for d in range(2 * k, layer_count)]
        )[None]
        for k in range(1, pairs)
    ]
    came = came[0] if pairs == 2 else jnp.concatenate(came, axis=0)
    dec_out = dec_grad(acts, grads)
    enc_out = enc_grad(own_term, came, active_mask[0], inputs)
    return (enc_out[None], dec_out[None], loss_tile.reshape(()))


def plain_step(
    resid_in, resid_out, token_ids, active_mask, enc_weight, enc_bias, dec_weight, dec_bias
):
    layer_count = lax.axis_size("layer")
    lat_count = lax.axis_size("lat")
    layer_here = lax.axis_index("layer")
    inputs_local = resid_in[0]
    wanted = resid_out[0]
    weight_enc = enc_weight[0]
    lat_rows = weight_enc.shape[0]
    feature_count = weight_enc.shape[1]
    feature_rows, token_count = inputs_local.shape
    total_cells = feature_count * token_count
    kept_tokens = (token_ids != 128000).astype(F32)
    source_ids = jnp.arange(layer_count)
    gating = active_mask[0].astype(F32)
    weight_rows = dec_weight[0].reshape(layer_count * lat_rows, feature_count)
    whole_inputs, target_stats = gather_inputs(inputs_local, wanted, lat_count)
    whole_inputs = whole_inputs.reshape(feature_count, token_count)
    spread = jnp.sum(target_stats[:, 0, 0]) / total_cells + EPSILON
    preact = jnp.dot(weight_enc, whole_inputs, preferred_element_type=F32)
    preact = preact + enc_bias[0].astype(F32)[:, None]
    latents = (gating * preact).astype(BF16)
    gathered = lax.all_gather(latents[None], "layer", axis=0, tiled=True)
    acts_stack = jnp.where(
        (source_ids <= layer_here)[:, None, None], gathered, jnp.zeros((), BF16)
    )
    stack_rows = acts_stack.reshape(layer_count * lat_rows, token_count)
    parts = lax.dot_general(
        weight_rows, stack_rows, (((0,), (0,)), ((), ())), preferred_element_type=F32
    ).astype(BF16)
    full_grad, err_stats = reduce_and_gather(
        parts.reshape(lat_count, feature_rows, token_count),
        wanted,
        dec_bias[0].astype(F32)[:, None],
        kept_tokens[None, :],
        jnp.broadcast_to(spread, (1, token_count)),
        lat_count,
    )
    full_grad = full_grad.reshape(feature_count, token_count)
    layer_loss = jnp.sum(err_stats[:, 0, 0]) / (2.0 * spread * total_cells)
    total_loss = lax.psum(layer_loss, "layer")
    grad_rows = jnp.dot(weight_rows, full_grad, preferred_element_type=F32).reshape(
        layer_count, lat_rows, token_count
    )
    grad_rows = (grad_rows * (source_ids <= layer_here).astype(F32)[:, None, None]).astype(BF16)
    dec_out = lax.dot_general(
        stack_rows, full_grad, (((1,), (1,)), ((), ())), preferred_element_type=F32
    )
    dec_out = dec_out.astype(BF16).reshape(1, layer_count, lat_rows, feature_count)
    latent_grad = lax.psum_scatter(grad_rows, "layer", scatter_dimension=0, tiled=True)[0]
    preact_grad = (gating * latent_grad.astype(F32)).astype(BF16)
    enc_out = lax.dot_general(
        preact_grad, whole_inputs, (((1,), (1,)), ((), ())), preferred_element_type=F32
    )
    return (enc_out.astype(BF16)[None], dec_out, total_loss)


def solution(mesh):
    in_specs = (
        P("layer", "lat", None),
        P("layer", "lat", None),
        P(),
        P("layer", "lat", None),
        P("layer", "lat", None),
        P("layer", "lat"),
        P("layer", None, "lat", None),
        P("layer", "lat"),
    )
    out_specs = (P("layer", "lat", None), P("layer", None, "lat", None), P())
    return jax.shard_map(
        on_device, mesh=mesh, in_specs=in_specs, out_specs=out_specs, check_vma=False
    )
```

```python
import functools

import jax
import jax.numpy as jnp
from jax import lax
from jax.experimental import pallas as pl
from jax.experimental.pallas import tpu as pltpu
from jax.sharding import PartitionSpec as P

EPSILON = 1e-05
F32 = jnp.float32
BF16 = jnp.bfloat16


class Place:
    def __init__(self, lat_count):
        self.me = lax.axis_index("lat")
        self.depth = lat_count // 2
        self.z = self.me // 2
        self.y = self.me % 2
        self.partner = self.me + 1 - 2 * self.y
        self.has_up = self.z < self.depth - 1
        self.has_down = self.z > 0


def send(src, dst, send_sem, recv_sem, lat):
    return pltpu.make_async_remote_copy(
        src_ref=src,
        dst_ref=dst,
        send_sem=send_sem,
        recv_sem=recv_sem,
        device_id={"lat": lat},
        device_id_type=pl.DeviceIdType.MESH,
    )


def greet(at, more=0):
    barrier = pltpu.get_barrier_semaphore()

    def hello(lat):
        pl.semaphore_signal(
            barrier, inc=1, device_id={"lat": lat}, device_id_type=pl.DeviceIdType.MESH
        )

    hello(at.partner)
    pl.when(at.has_up)(lambda: hello(at.me + 2))
    pl.when(at.has_down)(lambda: hello(at.me - 2))
    peers = 1 + more + at.has_up.astype(jnp.int32) + at.has_down.astype(jnp.int32)
    pl.semaphore_wait(barrier, peers)


class Gather:
    def __init__(self, at, own, whole, sems):
        self.at, self.own, self.whole, self.sems = at, own, whole, sems

    def hop(self, kind, d):
        at = self.at
        shard = at.me - 2 * d if kind in (0, 2) else at.me + 2 * d
        src = self.own if d == 0 else self.whole.at[shard]
        to = (at.me + 2, at.me - 2, at.partner, at.partner)[kind]
        later = d + 1 if kind < 2 else d
        return send(
            src, self.whole.at[shard], self.sems.at[0, kind, d], self.sems.at[1, kind, later], to
        )

    def landing(self, kind, d):
        at = self.at
        below = kind in (0, 2)
        shard = at.me - 2 * d if below else at.me + 2 * d
        if kind >= 2:
            shard = shard + 1 - 2 * at.y
        ref = self.whole.at[shard]
        return send(ref, ref, self.sems.at[0, kind, d], self.sems.at[1, kind, d], at.partner)

    def start(self):
        pl.when(self.at.has_up)(lambda: self.hop(0, 0).start())
        pl.when(self.at.has_down)(lambda: self.hop(1, 0).start())
        self.hop(2, 0).start()

    def step(self, d):
        at = self.at

        @pl.when(at.z >= d)
        def _():
            self.landing(0, d).wait_recv()
            pl.when(at.has_up)(lambda: self.hop(0, d).start())
            self.hop(2, d).start()

        @pl.when(at.z + d < at.depth)
        def _():
            self.landing(1, d).wait_recv()
            pl.when(at.has_down)(lambda: self.hop(1, d).start())
            self.hop(3, d).start()

    def finish(self, crossed=False):
        at = self.at
        for d in range(at.depth):

            @pl.when(at.z >= d)
            def _():
                if not crossed:
                    self.landing(2, d).wait_recv()
                self.hop(2, d).wait_send()
                if d < at.depth - 1:
                    pl.when(at.has_up)(lambda: self.hop(0, d).wait_send())

            @pl.when(at.z + d < at.depth)
            def _():
                if d > 0:
                    if not crossed:
                        self.landing(3, d).wait_recv()
                    self.hop(3, d).wait_send()
                if d < at.depth - 1:
                    pl.when(at.has_down)(lambda: self.hop(1, d).wait_send())


def gather_kernel(lat_count, own, wanted_ref, whole, stats, stat, big_sems, stat_sems, local_sem):
    at = Place(lat_count)
    greet(at)
    big = Gather(at, own, whole, big_sems)
    big.start()
    keep = pltpu.make_async_copy(own, whole.at[at.me], local_sem)
    keep.start()
    wanted = wanted_ref[...].astype(F32)
    centered = wanted - jnp.mean(wanted, axis=1, keepdims=True)
    total = jnp.sum(centered * centered, keepdims=True)
    stat[...] = jnp.broadcast_to(total, stat.shape)
    stats[at.me] = stat[...]
    small = Gather(at, stat, stats, stat_sems)
    small.start()
    for d in range(1, at.depth):
        big.step(d)
        small.step(d)
    keep.wait()
    big.finish()
    small.finish()


def reduce_kernel(
    lat_count,
    parts,
    wanted_ref,
    bias_ref,
    kept_ref,
    spread_ref,
    whole,
    stats,
    across_up,
    across_down,
    from_below,
    from_above,
    going_up,
    going_down,
    total,
    grad,
    stat,
    across_sems,
    line_sems,
    big_sems,
    stat_sems,
):
    at = Place(lat_count)
    depth = at.depth
    greet(at)

    def across(up, d):
        rung = at.z + d if up else at.z - d
        row = 0 if up else 1
        return send(
            parts.at[rung * 2 + 1 - at.y],
            (across_up if up else across_down).at[d],
            across_sems.at[0, row, d],
            across_sems.at[1, row, d],
            at.partner,
        )

    def along(up, d):
        row = 0 if up else 1
        return send(
            (going_up if up else going_down).at[d],
            (from_below if up else from_above).at[d - 1],
            line_sems.at[0, row, d],
            line_sems.at[1, row, d - 1],
            at.me + 2 if up else at.me - 2,
        )

    def arrived(up, d):
        row = 0 if up else 1
        ref = (from_below if up else from_above).at[d]
        send(ref, ref, line_sems.at[0, row, d], line_sems.at[1, row, d], at.partner).wait_recv()

    for d in range(depth - 1, -1, -1):
        pl.when(at.z + d < depth)(lambda: across(True, d).start())
        if d:
            pl.when(at.z >= d)(lambda: across(False, d).start())

    def forward(up, d):
        across(up, d).wait_recv()
        rung = at.z + d if up else at.z - d
        crossed = across_up if up else across_down
        came = from_below if up else from_above
        going = going_up if up else going_down
        behind = at.has_down if up else at.has_up
        mine = parts.at[rung * 2 + at.y]

        @pl.when(behind)
        def _():
            if d < depth - 1:
                arrived(up, d)
                going[d] = (
                    mine[...].astype(F32) + crossed[d].astype(F32) + came[d].astype(F32)
                ).astype(BF16)

        @pl.when(jnp.logical_not(behind))
        def _():
            going[d] = (mine[...].astype(F32) + crossed[d].astype(F32)).astype(BF16)

        along(up, d).start()

    for d in range(depth - 1, 0, -1):
        pl.when(at.z + d < depth)(lambda: forward(True, d))
        pl.when(at.z >= d)(lambda: forward(False, d))
    across(True, 0).wait_recv()
    total[...] = (
        parts[at.me].astype(F32)
        + across_up[0].astype(F32)
        + (bias_ref[...] - wanted_ref[...].astype(F32))
    )

    @pl.when(at.has_down)
    def _():
        arrived(True, 0)
        total[...] += from_below[0].astype(F32)

    @pl.when(at.has_up)
    def _():
        arrived(False, 0)
        total[...] += from_above[0].astype(F32)

    err = kept_ref[...] * total[...]
    grad[...] = (err / spread_ref[...]).astype(BF16)
    whole[at.me] = grad[...]
    big = Gather(at, grad, whole, big_sems)
    big.start()
    stat[...] = jnp.broadcast_to(jnp.sum(err * err, keepdims=True), stat.shape)
    stats[at.me] = stat[...]
    small = Gather(at, stat, stats, stat_sems)
    small.start()
    for d in range(1, depth):
        big.step(d)
        small.step(d)
    big.finish()
    small.finish()
    for d in range(depth - 1, -1, -1):

        @pl.when(at.z + d < depth)
        def _():
            across(True, d).wait_send()
            if d:
                along(True, d).wait_send()

        if d:

            @pl.when(at.z >= d)
            def _():
                across(False, d).wait_send()
                along(False, d).wait_send()


def to_layer(src, dst, send_sem, recv_sem, layer):
    return pltpu.make_async_remote_copy(
        src_ref=src,
        dst_ref=dst,
        send_sem=send_sem,
        recv_sem=recv_sem,
        device_id={"layer": layer},
        device_id_type=pl.DeviceIdType.MESH,
    )


class Spread:
    def __init__(self, at, ref, sems, pair_sems):
        self.at, self.ref, self.sems, self.pair_sems = at, ref, sems, pair_sems

    def shard_of(self, kind, d, landing=False):
        at = self.at
        shard = at.me - 2 * d if kind in (0, 2) else at.me + 2 * d
        if landing and kind >= 2:
            shard = shard + 1 - 2 * at.y
        return shard

    def hop(self, kind, d):
        at = self.at
        ref = self.ref(self.shard_of(kind, d))
        later = d + 1 if kind < 2 else d
        to = (at.me + 2, at.me - 2, at.partner, at.partner)[kind]
        return send(ref, ref, self.sems.at[0, kind, d], self.sems.at[1, kind, later], to)

    def landing(self, kind, d):
        ref = self.ref(self.shard_of(kind, d, True))
        return send(
            ref, ref, self.sems.at[0, kind, d], self.sems.at[1, kind, d], self.at.partner
        )

    def crossing(self, what, kind, d, act):
        if d != 1 or self.pair_sems is None:
            act(what(kind, d))
            return
        straight = jnp.logical_not(self.at.odd) if kind == 2 else self.at.odd
        pl.when(straight)(lambda: act(what(kind, d)))

    def aside(self, landing=False):
        at = self.at
        ref = self.ref(at.beside + 1 - 2 * at.y if landing else at.partner)
        return send(ref, ref, self.pair_sems.at[0], self.pair_sems.at[1], at.beside)

    def start(self):
        self.hop(2, 0).start()
        pl.when(self.at.has_up)(lambda: self.hop(0, 0).start())
        pl.when(self.at.has_down)(lambda: self.hop(1, 0).start())

    def line(self, d):
        at = self.at

        @pl.when(at.z >= d)
        def _():
            self.landing(0, d).wait_recv()
            pl.when(at.has_up)(lambda: self.hop(0, d).start())
            self.crossing(self.hop, 2, d, lambda one: one.start())

        @pl.when(at.z + d < at.depth)
        def _():
            self.landing(1, d).wait_recv()
            pl.when(at.has_down)(lambda: self.hop(1, d).start())
            self.crossing(self.hop, 3, d, lambda one: one.start())

    def settle(self, d):
        at = self.at
        if d == 0:
            self.landing(2, 0).wait_recv()
            if self.pair_sems is not None:
                self.aside().start()
            return
        if d == 1 and self.pair_sems is not None:
            self.aside(True).wait_recv()
        arrive = lambda one: one.wait_recv()
        pl.when(at.z >= d)(lambda: self.crossing(self.landing, 2, d, arrive))
        pl.when(at.z + d < at.depth)(lambda: self.crossing(self.landing, 3, d, arrive))

    def finish(self):
        at = self.at
        if self.pair_sems is not None:
            self.aside().wait_send()
        for d in range(at.depth):

            @pl.when(at.z >= d)
            def _():
                self.crossing(self.hop, 2, d, lambda one: one.wait_send())
                if d < at.depth - 1:
                    pl.when(at.has_up)(lambda: self.hop(0, d).wait_send())

            @pl.when(at.z + d < at.depth)
            def _():
                if d > 0:
                    self.crossing(self.hop, 3, d, lambda one: one.wait_send())
                if d < at.depth - 1:
                    pl.when(at.has_down)(lambda: self.hop(1, d).wait_send())


def advance(at, *stages):
    for group, d, use in stages:
        if 0 < d < at.depth:
            for one in group:
                one.line(d)
    for group, d, use in stages:
        if d == 0:
            for one in group:
                one.start()
    for group, d, use in stages:
        if d == 1:
            use(at.me)
        if 0 < d < at.depth:
            both_ways(at, at.me, d, use)
    for group, d, use in stages:
        if d > 0:
            for one in group:
                one.settle(d - 1)
    for group, d, use in stages:
        if d == 1:
            use(at.partner)
        if d > 1:
            both_ways(at, at.partner, d - 1, use)


def reaches(at, step):
    return jnp.logical_and(at.z + step >= 0, at.z + step < at.depth)


def both_ways(at, start, d, use):
    @pl.loop(0, 2)
    def _(row):
        step = (1 - 2 * row) * d
        pl.when(reaches(at, step))(lambda: use(start + 2 * step))


def step_kernel(
    lat_count,
    own,
    wanted_ref,
    enc_weight,
    enc_bias,
    gate_ref,
    dec_weight,
    dec_bias,
    ids_ref,
    turned_x_out,
    grads_out,
    acts_out,
    own_term_out,
    terms_out,
    loss,
    whole_x,
    turned_x,
    wanted_here,
    gate_here,
    enc_blocks,
    acc_enc,
    acts,
    turned,
    blocks,
    base,
    kept,
    leaving,
    crossed,
    came,
    going,
    pair_in,
    fresh,
    whole_g,
    column,
    acc,
    giving,
    given,
    terms,
    losses,
    spread_tile,
    stats,
    x_sems,
    x_pair_sems,
    g_sems,
    g_pair_sems,
    across_sems,
    line_sems,
    pair_sems,
    layer_sems,
    mate_sems,
    loss_sems,
    stat_sems,
    enc_sems,
    block_sems,
    local_sems,
    out_sems,
):
    at = Place(lat_count)
    at.odd = at.z % 2 == 1
    at.beside = at.me + 2 - 4 * (at.z % 2)
    depth = at.depth
    layer_count = acts.shape[1]
    rows, half = whole_x.shape[2:]
    piece = half // 2
    layer = lax.axis_index("layer")
    pairs = layer_count // 2
    pair, core = layer // 2, layer % 2
    mate = layer + 1 - 2 * core
    cells = lat_count * rows * half * 2

    def own_half(h):
        return pltpu.make_async_copy(
            own.at[:, pl.ds(h * half, half)], whole_x.at[h, at.me], local_sems.at[h]
        )

    def load_enc(g):
        return pltpu.make_async_copy(
            enc_weight.at[:, pl.ds(g * rows, rows)], enc_blocks.at[g], enc_sems.at[g]
        )

    def load_dec(g):
        return pltpu.make_async_copy(
            dec_weight.at[:, :, pl.ds(g * rows, rows)], blocks.at[g], block_sems.at[g]
        )

    fetch = pltpu.make_async_copy(wanted_ref, wanted_here, local_sems.at[2])
    fetch_gate = pltpu.make_async_copy(gate_ref, gate_here, local_sems.at[3])
    own_half(0).start()
    own_half(1).start()
    for g in range(lat_count):
        load_enc(g).start()
    fetch.start()
    fetch_gate.start()

    barrier = pltpu.get_barrier_semaphore()
    for k in range(1, layer_count):
        other = lax.rem(layer + k, layer_count)
        pl.semaphore_signal(
            barrier, inc=1, device_id={"layer": other}, device_id_type=pl.DeviceIdType.MESH
        )
    own_half(0).wait()
    own_half(1).wait()
    greet(at, layer_count - 1)

    def tally(which):
        return Spread(at, lambda shard: stats.at[which, shard], stat_sems.at[which], None)

    def feature_piece(h, q):
        def ref(shard):
            return whole_x.at[h, shard, pl.ds(q * (rows // 2), rows // 2)]

        return Spread(at, ref, x_sems.at[h, q], x_pair_sems.at[h] if q else None)

    def use_x(h):
        def use(g):
            acc_enc[h] += jnp.dot(enc_blocks[g], whole_x[h, g], preferred_element_type=F32)

        return use

    gather_x = [[feature_piece(h, q) for q in range(2)] for h in range(2)]
    gather_x.append([tally(0)])

    def stage_x(*which):
        uses = use_x(0), use_x(1), lambda g: None
        advance(at, *[(gather_x[h], d, uses[h]) for h, d in which])

    stage_x((0, 0))
    bias = jnp.transpose(jnp.broadcast_to(enc_bias[...].astype(F32), (half, enc_bias.shape[1])))
    acc_enc[0] = bias
    acc_enc[1] = bias
    turned[...] = jnp.zeros_like(turned)
    for g in range(lat_count):
        load_enc(g).wait()
    for g in range(lat_count):
        load_dec(g).start()
    stage_x((0, 1), (1, 0))
    fetch.wait()
    wanted = wanted_here[...].astype(F32)
    centered = wanted - jnp.mean(wanted, axis=1, keepdims=True)
    total = jnp.sum(centered * centered, keepdims=True)
    stats[0, at.me] = jnp.broadcast_to(total, stats.shape[2:])
    stage_x((0, 2), (1, 1), (2, 0))
    stage_x((0, 3), (1, 2), (2, 1))
    base[...] = dec_bias[...].astype(F32) - jnp.transpose(wanted_here[...].astype(F32))
    fetch_gate.wait()
    stage_x((0, 4), (2, 2))

    def over(h, k):
        ref = acts.at[h, layer]
        return to_layer(
            ref, ref, layer_sems.at[0, h, 0, k], layer_sems.at[1, h, 0, k], layer + 2 * k
        )

    def pass_on(h, k):
        ref = acts.at[h, layer - 2 * k]
        return to_layer(ref, ref, layer_sems.at[0, h, 1, k], layer_sems.at[1, h, 1, k], mate)

    def landed(h, kind, k):
        ref = acts.at[h, layer - 2 * k if kind == 0 else mate - 2 * k]
        sem = layer_sems.at[1, h, kind, k]
        return to_layer(ref, ref, layer_sems.at[0, h, kind, k], sem, mate)

    def turn(h, source):
        turned[source, h * half : (h + 1) * half] = jnp.transpose(acts[h, source])

    def exchange(h):
        gate = gate_here[:, h * half : (h + 1) * half].astype(F32)
        acts[h, layer] = (gate * acc_enc[h]).astype(BF16)
        for k in range(1, pairs):
            pl.when(pair + k < pairs)(lambda: over(h, k).start())
        pl.when(core == 0)(lambda: pass_on(h, 0).start())
        turn(h, layer)
        yield
        for k in range(1, pairs):

            @pl.when(pair >= k)
            def _():
                landed(h, 0, k).wait_recv()
                pass_on(h, k).start()
                turn(h, layer - 2 * k)

        yield

        @pl.when(core == 1)
        def _():
            landed(h, 1, 0).wait_recv()
            turn(h, mate)

        for k in range(1, pairs):

            @pl.when(pair >= k)
            def _():
                landed(h, 1, k).wait_recv()
                turn(h, mate - 2 * k)

        yield

    def exchange_sent(h):
        pl.when(core == 0)(lambda: pass_on(h, 0).wait_send())
        for k in range(1, pairs):
            pl.when(pair >= k)(lambda: pass_on(h, k).wait_send())
            pl.when(pair + k < pairs)(lambda: over(h, k).wait_send())

    moves = [exchange(h) for h in range(2)]
    next(moves[0])
    stage_x((1, 3), (2, 3))
    next(moves[0])
    stage_x((1, 4), (2, 4))
    next(moves[1])
    next(moves[0])
    for g in range(lat_count):
        load_dec(g).wait()
    spread_tile[...] = jnp.sum(stats[0], axis=0) / cells + EPSILON
    spread = jnp.max(spread_tile[...], keepdims=True)

    def part(h, g):
        some = slice(h * half, (h + 1) * half)
        got = jnp.dot(turned[0, some], blocks[g, 0], preferred_element_type=F32)
        for source in range(1, layer_count):
            got += jnp.dot(turned[source, some], blocks[g, source], preferred_element_type=F32)
        fresh[...] = got

    def within(p):
        return pl.ds(p % 2 * piece, piece)

    def of(p):
        return pl.ds(p * piece, piece)

    def across(p, row, d):
        return send(
            leaving.at[row, d, of(p)],
            crossed.at[row, d, of(p)],
            across_sems.at[0, p, row, d],
            across_sems.at[1, p, row, d],
            at.partner,
        )

    def aside(p, row):
        return send(
            leaving.at[row, 1, of(p)],
            pair_in.at[p // 2],
            pair_sems.at[0, p // 2],
            pair_sems.at[1, p // 2],
            at.beside,
        )

    def by_side(p, row, d, cross, turn_aside=None):
        if d != 1 or p % 2 == 0:
            cross()
            return
        beside = lax.rem(at.z + row, 2) == 0
        pl.when(jnp.logical_not(beside))(cross)
        if turn_aside is not None:
            pl.when(beside)(turn_aside)

    def along(p, row, d):
        return send(
            going.at[row, d, of(p)],
            came.at[row, d - 1, of(p)],
            line_sems.at[0, p, row, d],
            line_sems.at[1, p, row, d - 1],
            at.me + 2 - 4 * row,
        )

    def arrived(p, row, d):
        ref = came.at[row, d, of(p)]
        sems = line_sems.at[0, p, row, d], line_sems.at[1, p, row, d]
        send(ref, ref, *sems, at.partner).wait_recv()
        fresh[within(p), :] += came[row, d, of(p)].astype(F32)

    def met(p, row, d):
        across(p, row, d).wait_recv()
        fresh[within(p), :] += crossed[row, d, of(p)].astype(F32)

    def leave(h, row, d):
        part(h, at.partner + 2 * d * (1 - 2 * row))
        if d == 0:
            aside(2 * h + 1, 0).wait_recv()
            fresh[piece:] += pair_in[h].astype(F32)
        leaving[row, d, h * half : (h + 1) * half] = fresh[...].astype(BF16)
        for p in (2 * h, 2 * h + 1):
            by_side(
                p, row, d, lambda: across(p, row, d).start(), lambda: aside(p, row).start()
            )

    def leaves(h, d):
        if d == 0:
            leave(h, 0, 0)
            return

        @pl.loop(0, 2)
        def _(row):
            pl.when(reaches(at, d * (1 - 2 * row)))(lambda: leave(h, row, d))

    def forward(h, row, d):
        part(h, at.me + 2 * d * (1 - 2 * row))
        for p in (2 * h, 2 * h + 1):
            by_side(p, row, d, lambda: met(p, row, d))
            if d < depth - 1:
                pl.when(reaches(at, 2 * row - 1))(lambda: arrived(p, row, d))
            going[row, d, of(p)] = fresh[within(p), :].astype(BF16)
            along(p, row, d).start()

    def forwards(h, d):
        @pl.loop(0, 2)
        def _(row):
            pl.when(reaches(at, d * (1 - 2 * row)))(lambda: forward(h, row, d))

    def token_piece(p):
        def ref(shard):
            return whole_g.at[shard, of(p)]

        return Spread(at, ref, g_sems.at[p], g_pair_sems.at[p // 2] if p % 2 else None)

    gather_g = [token_piece(p) for p in range(4)]
    gather_g.append(tally(1))

    def use_g(g):
        column[...] = jnp.transpose(whole_g[g])
        for source in range(layer_count):
            acc[source] += jnp.dot(blocks[g, source], column[...], preferred_element_type=F32)

    def close(h):
        part(h, at.me)
        fresh[...] += base[h * half : (h + 1) * half]
        for p in (2 * h, 2 * h + 1):
            met(p, 0, 0)
            pl.when(at.has_down)(lambda: arrived(p, 0, 0))
            pl.when(at.has_up)(lambda: arrived(p, 1, 0))
            err = kept[of(p), :1] * fresh[within(p), :]
            whole_g[at.me, of(p)] = (err / spread).astype(BF16)
            gather_g[p].start()
            total = jnp.sum(err * err, keepdims=True)
            if p == 0:
                stats[1, at.me] = jnp.broadcast_to(total, stats.shape[2:])
            else:
                stats[1, at.me] += total
        if h:
            gather_g[4].start()

    def turn_x(g):
        for h in range(2):
            turned_x[g, h * half : (h + 1) * half] = jnp.transpose(whole_x[h, g])

    def stage_g(*which):
        uses = turn_x, use_g
        advance(at, *[(gather_g[2 * h : 2 * h + 2 + h], d, uses[h]) for h, d in which])

    leaves(0, 3)
    leaves(0, 2)
    leaves(0, 1)
    next(moves[1])
    forwards(0, 3)
    next(moves[1])
    leaves(1, 3)
    forwards(0, 2)
    leaves(1, 2)
    leaves(0, 0)
    forwards(0, 1)
    leaves(1, 1)
    forwards(1, 3)
    ids = jnp.broadcast_to((ids_ref[...] != 128000).astype(F32), (128, 2 * half))
    kept[...] = jnp.transpose(ids)
    close(0)
    forwards(1, 2)
    leaves(1, 0)
    stage_g((0, 1))
    forwards(1, 1)
    stage_g((0, 2))
    acc[...] = jnp.zeros_like(acc)
    close(1)
    stage_g((0, 3), (1, 1))
    stage_g((0, 4), (1, 2))
    stage_g((1, 3))

    def out(which):
        src, dst = (
            (turned_x, turned_x_out),
            (acts, acts_out),
            (whole_g, grads_out),
            (acc.at[layer], own_term_out),
            (terms, terms_out),
        )[which]
        return pltpu.make_async_copy(src, dst, out_sems.at[which])

    out(0).start()
    out(1).start()
    stage_g((1, 4))
    out(2).start()
    losses[layer] = jnp.sum(stats[1], axis=0) / (2.0 * spread_tile[...] * cells)

    def tell(k, told=False):
        other = lax.rem(layer + (layer_count - k if told else k), layer_count)
        ref = losses.at[other if told else layer]
        return to_layer(ref, ref, loss_sems.at[0, k], loss_sems.at[1, k], other)

    def give(k):
        return to_layer(
            giving.at[k], given.at[k], mate_sems.at[0, k], mate_sems.at[1, k], mate
        )

    def hand(k):
        giving[k] = acc[mate - 2 * k].astype(BF16)
        give(k).start()

    for k in range(pairs - 1, 0, -1):
        pl.when(pair >= k)(lambda: hand(k))
    pl.when(core == 1)(lambda: hand(0))
    for k in range(1, layer_count):
        tell(k).start()
    for k in range(pairs - 1, 0, -1):

        @pl.when(pair >= k)
        def _():
            give(k).wait_recv()
            terms[k - 1] = (acc[layer - 2 * k] + given[k].astype(F32)).astype(BF16)
            give(k).wait_send()

        @pl.when(pair < k)
        def _():
            terms[k - 1] = jnp.zeros(terms.shape[1:], BF16)

    out(4).start()

    @pl.when(core == 0)
    def _():
        give(0).wait_recv()
        acc[layer] += given[0].astype(F32)

    out(3).start()
    pl.when(core == 1)(lambda: give(0).wait_send())
    for k in range(1, layer_count):
        tell(k, True).wait_recv()
        tell(k).wait_send()
    loss[...] = jnp.sum(losses[...], axis=0)[:1, :1]
    for group in gather_x:
        for one in group:
            one.finish()
    for h in range(2):
        exchange_sent(h)
    for one in gather_g:
        one.finish()
    for p in range(4):
        if p % 2:
            aside(p, 0).wait_send()
        for d in range(depth):
            for row in range(2):
                if d or row == 0:

                    @pl.when(reaches(at, d * (1 - 2 * row)))
                    def _():
                        by_side(p, row, d, lambda: across(p, row, d).wait_send())
                        if d:
                            along(p, row, d).wait_send()

    for which in range(5):
        out(which).wait()


VMEM = pl.BlockSpec(memory_space=pltpu.VMEM)
HBM = pl.BlockSpec(memory_space=pltpu.HBM)


def step(inputs_local, wanted, enc_weight, enc_bias, gate, dec_weight, dec_bias, ids, lat_count):
    rows, tokens = inputs_local.shape
    layer_count, lat_rows, _ = dec_weight.shape
    depth = lat_count // 2
    pairs = layer_count // 2
    half = tokens // 2
    slots = pltpu.VMEM((2, depth, tokens, rows), BF16)
    dma = pltpu.SemaphoreType.DMA
    return pl.pallas_call(
        functools.partial(step_kernel, lat_count),
        out_shape=(
            jax.ShapeDtypeStruct((lat_count, tokens, rows), BF16),
            jax.ShapeDtypeStruct((lat_count, tokens, rows), BF16),
            jax.ShapeDtypeStruct((2, layer_count, lat_rows, half), BF16),
            jax.ShapeDtypeStruct((lat_rows, tokens), F32),
            jax.ShapeDtypeStruct((pairs - 1, lat_rows, tokens), BF16),
            jax.ShapeDtypeStruct((1, 1), F32),
        ),
        in_specs=[HBM, HBM, HBM, VMEM, HBM, HBM, VMEM, VMEM],
        out_specs=(HBM,) * 5 + (VMEM,),
        scratch_shapes=[
            pltpu.VMEM((2, lat_count, rows, half), BF16),
            pltpu.VMEM((lat_count, tokens, rows), BF16),
            pltpu.VMEM((rows, tokens), BF16),
            pltpu.VMEM((lat_rows, tokens), jnp.int32),
            pltpu.VMEM((lat_count, lat_rows, rows), BF16),
            pltpu.VMEM((2, lat_rows, half), F32),
            pltpu.VMEM((2, layer_count, lat_rows, half), BF16),
            pltpu.VMEM((layer_count, tokens, lat_rows), BF16),
            pltpu.VMEM((lat_count, layer_count, lat_rows, rows), BF16),
            pltpu.VMEM((tokens, rows), F32),
            pltpu.VMEM((tokens, 128), F32),
        ]
        + [slots] * 4
        + [
            pltpu.VMEM((2, half // 2, rows), BF16),
            pltpu.VMEM((half, rows), F32),
            pltpu.VMEM((lat_count, tokens, rows), BF16),
            pltpu.VMEM((rows, tokens), BF16),
            pltpu.VMEM((layer_count, lat_rows, tokens), F32),
            pltpu.VMEM((pairs, lat_rows, tokens), BF16),
            pltpu.VMEM((pairs, lat_rows, tokens), BF16),
            pltpu.VMEM((pairs - 1, lat_rows, tokens), BF16),
            pltpu.VMEM((layer_count, 8, 128), F32),
            pltpu.VMEM((8, 128), F32),
            pltpu.VMEM((2, lat_count, 8, 128), F32),
            dma((2, 2, 2, 4, depth + 1)),
            dma((2, 2)),
            dma((4, 2, 4, depth + 1)),
            dma((2, 2)),
            dma((2, 4, 2, depth)),
            dma((2, 4, 2, depth)),
            dma((2, 2)),
            dma((2, 2, 2, pairs)),
            dma((2, pairs)),
            dma((2, layer_count)),
            dma((2, 2, 4, depth + 1)),
            dma((lat_count,)),
            dma((lat_count,)),
            dma((4,)),
            dma((5,)),
        ],
        compiler_params=pltpu.CompilerParams(
            collective_id=2, has_side_effects=True, vmem_limit_bytes=60 << 20
        ),
    )(inputs_local, wanted, enc_weight, enc_bias, gate, dec_weight, dec_bias, ids)


def dec_grad_kernel(acts_ref, grads_ref, out, acts, grads, ring, in_sems, out_sems):
    layer = lax.axis_index("layer")
    slots, block, _ = ring.shape
    _, layer_count, lat_rows, _ = acts.shape
    lat_count, _, rows = grads.shape
    parts = lat_rows // block
    count = layer_count * parts
    def fetch_acts(source):
        return pltpu.make_async_copy(
            acts_ref.at[:, source], acts.at[:, source], in_sems.at[lat_count + source]
        )

    def fetch_grads(g):
        return pltpu.make_async_copy(grads_ref.at[g], grads.at[g], in_sems.at[g])

    fetch_acts(0).start()
    for g in range(lat_count):
        fetch_grads(g).start()
    for source in range(1, layer_count):
        fetch_acts(source).start()
    fetch_acts(0).wait()

    def write(i):
        here = pl.ds(lax.rem(i, parts) * block, block)
        slot = lax.rem(i, slots)
        return pltpu.make_async_copy(
            ring.at[slot], out.at[lax.div(i, parts), here], out_sems.at[slot]
        )

    def made(i, g):
        source, here = lax.div(i, parts), pl.ds(lax.rem(i, parts) * block, block)
        left = jnp.concatenate([acts[0, source, here], acts[1, source, here]], axis=1)
        return jnp.dot(left, grads[g], preferred_element_type=F32).astype(BF16)

    for g in range(lat_count):
        if g % (lat_count // 2) == 0:
            for later in range(g, g + lat_count // 2):
                fetch_grads(later).wait()
        ring[0, :, g * rows : (g + 1) * rows] = made(0, g)
    write(0).start()
    for source in range(1, layer_count):
        fetch_acts(source).wait()

    @pl.loop(1, count)
    def _(i):
        pl.when(i >= slots)(lambda: write(i - slots).wait())
        source, slot = lax.div(i, parts), lax.rem(i, slots)

        @pl.when(source <= layer)
        def _():
            for g in range(lat_count):
                ring[slot, :, g * rows : (g + 1) * rows] = made(i, g)

        @pl.when(source > layer)
        def _():
            ring[slot] = jnp.zeros(ring.shape[1:], BF16)

        write(i).start()

    for i in range(max(count - slots, 0), count):
        write(i).wait()


def dec_grad(acts, grads):
    _, layer_count, lat_rows, half = acts.shape
    lat_count, tokens, rows = grads.shape
    features = lat_count * rows
    block = lat_rows // 2
    return pl.pallas_call(
        dec_grad_kernel,
        out_shape=jax.ShapeDtypeStruct((layer_count, lat_rows, features), BF16),
        in_specs=[HBM, HBM],
        out_specs=HBM,
        scratch_shapes=[
            pltpu.VMEM(acts.shape, BF16),
            pltpu.VMEM(grads.shape, BF16),
            pltpu.VMEM((3, block, features), BF16),
            pltpu.SemaphoreType.DMA((lat_count + layer_count,)),
            pltpu.SemaphoreType.DMA((3,)),
        ],
        cost_estimate=pl.CostEstimate(
            flops=2 * layer_count * lat_rows * tokens * features,
            bytes_accessed=2 * layer_count * lat_rows * features,
            transcendentals=0,
        ),
        compiler_params=pltpu.CompilerParams(vmem_limit_bytes=60 << 20),
    )(acts, grads)


def enc_grad_kernel(term, came, gate, inputs, out):
    total = term[...]
    for k in range(came.shape[0]):
        total = total + came[k].astype(F32)
    left = (gate[...].astype(F32) * total).astype(BF16)
    lat_count, _, rows = inputs.shape
    for g in range(lat_count):
        made = jnp.dot(left, inputs[g], preferred_element_type=F32)
        out[:, g * rows : (g + 1) * rows] = made.astype(BF16)


def enc_grad(term, came, gate, inputs):
    lat_rows, tokens = term.shape
    lat_count, _, rows = inputs.shape
    block = lat_rows // 4
    return pl.pallas_call(
        enc_grad_kernel,
        grid=(4,),
        out_shape=jax.ShapeDtypeStruct((lat_rows, lat_count * rows), BF16),
        in_specs=[
            pl.BlockSpec((block, tokens), lambda r: (r, 0)),
            pl.BlockSpec((came.shape[0], block, tokens), lambda r: (0, r, 0)),
            pl.BlockSpec((block, tokens), lambda r: (r, 0)),
            pl.BlockSpec(inputs.shape, lambda r: (0, 0, 0)),
        ],
        out_specs=pl.BlockSpec((block, lat_count * rows), lambda r: (r, 0)),
        compiler_params=pltpu.CompilerParams(vmem_limit_bytes=32 << 20),
    )(term, came, gate, inputs)


def gather_inputs(inputs_local, wanted, lat_count):
    rows, tokens = inputs_local.shape
    depth = lat_count // 2
    return pl.pallas_call(
        functools.partial(gather_kernel, lat_count),
        out_shape=(
            jax.ShapeDtypeStruct((lat_count, rows, tokens), BF16),
            jax.ShapeDtypeStruct((lat_count, 8, 128), F32),
        ),
        in_specs=[VMEM] * 2,
        out_specs=(VMEM, VMEM),
        scratch_shapes=[
            pltpu.VMEM((8, 128), F32),
            pltpu.SemaphoreType.DMA((2, 4, depth + 1)),
            pltpu.SemaphoreType.DMA((2, 4, depth + 1)),
            pltpu.SemaphoreType.DMA,
        ],
        compiler_params=pltpu.CompilerParams(
            collective_id=0, has_side_effects=True, vmem_limit_bytes=32 << 20
        ),
    )(inputs_local, wanted)


def reduce_and_gather(parts, wanted, bias, kept, spread, lat_count):
    _, rows, tokens = parts.shape
    depth = lat_count // 2
    slots = pltpu.VMEM((depth, rows, tokens), BF16)
    return pl.pallas_call(
        functools.partial(reduce_kernel, lat_count),
        out_shape=(
            jax.ShapeDtypeStruct((lat_count, rows, tokens), BF16),
            jax.ShapeDtypeStruct((lat_count, 8, 128), F32),
        ),
        in_specs=[VMEM] * 5,
        out_specs=(VMEM, VMEM),
        scratch_shapes=[slots] * 6
        + [
            pltpu.VMEM((rows, tokens), F32),
            pltpu.VMEM((rows, tokens), BF16),
            pltpu.VMEM((8, 128), F32),
            pltpu.SemaphoreType.DMA((2, 2, depth)),
            pltpu.SemaphoreType.DMA((2, 2, depth)),
            pltpu.SemaphoreType.DMA((2, 4, depth + 1)),
            pltpu.SemaphoreType.DMA((2, 4, depth + 1)),
        ],
        compiler_params=pltpu.CompilerParams(
            collective_id=1, has_side_effects=True, vmem_limit_bytes=40 << 20
        ),
    )(parts, wanted, bias, kept, spread)


def on_device(
    resid_in, resid_out, token_ids, active_mask, enc_weight, enc_bias, dec_weight, dec_bias
):
    layer_count = lax.axis_size("layer")
    lat_count = lax.axis_size("lat")
    lat_rows = enc_weight.shape[1]
    feature_rows, token_count = resid_in.shape[1:]
    fused = feature_rows % 128 == 0 and lat_rows % 128 == 0 and token_count == 256
    fused = fused and layer_count % 2 == 0 and layer_count > 2 and lat_count == 8
    args = (
        resid_in, resid_out, token_ids, active_mask, enc_weight, enc_bias, dec_weight, dec_bias
    )
    return fused_step(*args) if fused else plain_step(*args)


def fused_step(
    resid_in, resid_out, token_ids, active_mask, enc_weight, enc_bias, dec_weight, dec_bias
):
    layer_count = lax.axis_size("layer")
    pairs = layer_count // 2
    inputs, grads, acts, own_term, terms, loss_tile = step(
        resid_in[0],
        resid_out[0],
        enc_weight[0],
        enc_bias,
        active_mask[0],
        dec_weight[0],
        dec_bias,
        token_ids[None, :],
        lax.axis_size("lat"),
    )
    came = [
        lax.ppermute(
            terms[k - 1], "layer", [(d, d - 2 * k) for d in range(2 * k, layer_count)]
        )[None]
        for k in range(1, pairs)
    ]
    came = came[0] if pairs == 2 else jnp.concatenate(came, axis=0)
    dec_out = dec_grad(acts, grads)
    enc_out = enc_grad(own_term, came, active_mask[0], inputs)
    return (enc_out[None], dec_out[None], loss_tile.reshape(()))


def plain_step(
    resid_in, resid_out, token_ids, active_mask, enc_weight, enc_bias, dec_weight, dec_bias
):
    layer_count = lax.axis_size("layer")
    lat_count = lax.axis_size("lat")
    layer_here = lax.axis_index("layer")
    inputs_local = resid_in[0]
    wanted = resid_out[0]
    weight_enc = enc_weight[0]
    lat_rows = weight_enc.shape[0]
    feature_count = weight_enc.shape[1]
    feature_rows, token_count = inputs_local.shape
    total_cells = feature_count * token_count
    kept_tokens = (token_ids != 128000).astype(F32)
    source_ids = jnp.arange(layer_count)
    gating = active_mask[0].astype(F32)
    weight_rows = dec_weight[0].reshape(layer_count * lat_rows, feature_count)
    whole_inputs, target_stats = gather_inputs(inputs_local, wanted, lat_count)
    whole_inputs = whole_inputs.reshape(feature_count, token_count)
    spread = jnp.sum(target_stats[:, 0, 0]) / total_cells + EPSILON
    preact = jnp.dot(weight_enc, whole_inputs, preferred_element_type=F32)
    preact = preact + enc_bias[0].astype(F32)[:, None]
    latents = (gating * preact).astype(BF16)
    gathered = lax.all_gather(latents[None], "layer", axis=0, tiled=True)
    acts_stack = jnp.where(
        (source_ids <= layer_here)[:, None, None], gathered, jnp.zeros((), BF16)
    )
    stack_rows = acts_stack.reshape(layer_count * lat_rows, token_count)
    parts = lax.dot_general(
        weight_rows, stack_rows, (((0,), (0,)), ((), ())), preferred_element_type=F32
    ).astype(BF16)
    full_grad, err_stats = reduce_and_gather(
        parts.reshape(lat_count, feature_rows, token_count),
        wanted,
        dec_bias[0].astype(F32)[:, None],
        kept_tokens[None, :],
        jnp.broadcast_to(spread, (1, token_count)),
        lat_count,
    )
    full_grad = full_grad.reshape(feature_count, token_count)
    layer_loss = jnp.sum(err_stats[:, 0, 0]) / (2.0 * spread * total_cells)
    total_loss = lax.psum(layer_loss, "layer")
    grad_rows = jnp.dot(weight_rows, full_grad, preferred_element_type=F32).reshape(
        layer_count, lat_rows, token_count
    )
    grad_rows = (grad_rows * (source_ids <= layer_here).astype(F32)[:, None, None]).astype(BF16)
    dec_out = lax.dot_general(
        stack_rows, full_grad, (((1,), (1,)), ((), ())), preferred_element_type=F32
    )
    dec_out = dec_out.astype(BF16).reshape(1, layer_count, lat_rows, feature_count)
    latent_grad = lax.psum_scatter(grad_rows, "layer", scatter_dimension=0, tiled=True)[0]
    preact_grad = (gating * latent_grad.astype(F32)).astype(BF16)
    enc_out = lax.dot_general(
        preact_grad, whole_inputs, (((1,), (1,)), ((), ())), preferred_element_type=F32
    )
    return (enc_out.astype(BF16)[None], dec_out, total_loss)


def solution(mesh):
    in_specs = (
        P("layer", "lat", None),
        P("layer", "lat", None),
        P(),
        P("layer", "lat", None),
        P("layer", "lat", None),
        P("layer", "lat"),
        P("layer", None, "lat", None),
        P("layer", "lat"),
    )
    out_specs = (P("layer", "lat", None), P("layer", None, "lat", None), P())
    return jax.shard_map(
        on_device, mesh=mesh, in_specs=in_specs, out_specs=out_specs, check_vma=False
    )
```

```python
import functools

import jax
import jax.numpy as jnp
from jax import lax
from jax.experimental import pallas as pl
from jax.experimental.pallas import tpu as pltpu
from jax.sharding import PartitionSpec as P

EPSILON = 1e-05
F32 = jnp.float32
BF16 = jnp.bfloat16


class Place:
    def __init__(self, lat_count):
        self.me = lax.axis_index("lat")
        self.depth = lat_count // 2
        self.z = self.me // 2
        self.y = self.me % 2
        self.partner = self.me + 1 - 2 * self.y
        self.has_up = self.z < self.depth - 1
        self.has_down = self.z > 0


def send(src, dst, send_sem, recv_sem, lat):
    return pltpu.make_async_remote_copy(
        src_ref=src,
        dst_ref=dst,
        send_sem=send_sem,
        recv_sem=recv_sem,
        device_id={"lat": lat},
        device_id_type=pl.DeviceIdType.MESH,
    )


def greet(at, more=0):
    barrier = pltpu.get_barrier_semaphore()

    def hello(lat):
        pl.semaphore_signal(
            barrier, inc=1, device_id={"lat": lat}, device_id_type=pl.DeviceIdType.MESH
        )

    hello(at.partner)
    pl.when(at.has_up)(lambda: hello(at.me + 2))
    pl.when(at.has_down)(lambda: hello(at.me - 2))
    peers = 1 + more + at.has_up.astype(jnp.int32) + at.has_down.astype(jnp.int32)
    pl.semaphore_wait(barrier, peers)


class Gather:
    def __init__(self, at, own, whole, sems):
        self.at, self.own, self.whole, self.sems = at, own, whole, sems

    def hop(self, kind, d):
        at = self.at
        shard = at.me - 2 * d if kind in (0, 2) else at.me + 2 * d
        src = self.own if d == 0 else self.whole.at[shard]
        to = (at.me + 2, at.me - 2, at.partner, at.partner)[kind]
        later = d + 1 if kind < 2 else d
        return send(
            src, self.whole.at[shard], self.sems.at[0, kind, d], self.sems.at[1, kind, later], to
        )

    def landing(self, kind, d):
        at = self.at
        below = kind in (0, 2)
        shard = at.me - 2 * d if below else at.me + 2 * d
        if kind >= 2:
            shard = shard + 1 - 2 * at.y
        ref = self.whole.at[shard]
        return send(ref, ref, self.sems.at[0, kind, d], self.sems.at[1, kind, d], at.partner)

    def start(self):
        pl.when(self.at.has_up)(lambda: self.hop(0, 0).start())
        pl.when(self.at.has_down)(lambda: self.hop(1, 0).start())
        self.hop(2, 0).start()

    def step(self, d):
        at = self.at

        @pl.when(at.z >= d)
        def _():
            self.landing(0, d).wait_recv()
            pl.when(at.has_up)(lambda: self.hop(0, d).start())
            self.hop(2, d).start()

        @pl.when(at.z + d < at.depth)
        def _():
            self.landing(1, d).wait_recv()
            pl.when(at.has_down)(lambda: self.hop(1, d).start())
            self.hop(3, d).start()

    def finish(self, crossed=False):
        at = self.at
        for d in range(at.depth):

            @pl.when(at.z >= d)
            def _():
                if not crossed:
                    self.landing(2, d).wait_recv()
                self.hop(2, d).wait_send()
                if d < at.depth - 1:
                    pl.when(at.has_up)(lambda: self.hop(0, d).wait_send())

            @pl.when(at.z + d < at.depth)
            def _():
                if d > 0:
                    if not crossed:
                        self.landing(3, d).wait_recv()
                    self.hop(3, d).wait_send()
                if d < at.depth - 1:
                    pl.when(at.has_down)(lambda: self.hop(1, d).wait_send())


def gather_kernel(lat_count, own, wanted_ref, whole, stats, stat, big_sems, stat_sems, local_sem):
    at = Place(lat_count)
    greet(at)
    big = Gather(at, own, whole, big_sems)
    big.start()
    keep = pltpu.make_async_copy(own, whole.at[at.me], local_sem)
    keep.start()
    wanted = wanted_ref[...].astype(F32)
    centered = wanted - jnp.mean(wanted, axis=1, keepdims=True)
    total = jnp.sum(centered * centered, keepdims=True)
    stat[...] = jnp.broadcast_to(total, stat.shape)
    stats[at.me] = stat[...]
    small = Gather(at, stat, stats, stat_sems)
    small.start()
    for d in range(1, at.depth):
        big.step(d)
        small.step(d)
    keep.wait()
    big.finish()
    small.finish()


def reduce_kernel(
    lat_count,
    parts,
    wanted_ref,
    bias_ref,
    kept_ref,
    spread_ref,
    whole,
    stats,
    across_up,
    across_down,
    from_below,
    from_above,
    going_up,
    going_down,
    total,
    grad,
    stat,
    across_sems,
    line_sems,
    big_sems,
    stat_sems,
):
    at = Place(lat_count)
    depth = at.depth
    greet(at)

    def across(up, d):
        rung = at.z + d if up else at.z - d
        row = 0 if up else 1
        return send(
            parts.at[rung * 2 + 1 - at.y],
            (across_up if up else across_down).at[d],
            across_sems.at[0, row, d],
            across_sems.at[1, row, d],
            at.partner,
        )

    def along(up, d):
        row = 0 if up else 1
        return send(
            (going_up if up else going_down).at[d],
            (from_below if up else from_above).at[d - 1],
            line_sems.at[0, row, d],
            line_sems.at[1, row, d - 1],
            at.me + 2 if up else at.me - 2,
        )

    def arrived(up, d):
        row = 0 if up else 1
        ref = (from_below if up else from_above).at[d]
        send(ref, ref, line_sems.at[0, row, d], line_sems.at[1, row, d], at.partner).wait_recv()

    for d in range(depth - 1, -1, -1):
        pl.when(at.z + d < depth)(lambda: across(True, d).start())
        if d:
            pl.when(at.z >= d)(lambda: across(False, d).start())

    def forward(up, d):
        across(up, d).wait_recv()
        rung = at.z + d if up else at.z - d
        crossed = across_up if up else across_down
        came = from_below if up else from_above
        going = going_up if up else going_down
        behind = at.has_down if up else at.has_up
        mine = parts.at[rung * 2 + at.y]

        @pl.when(behind)
        def _():
            if d < depth - 1:
                arrived(up, d)
                going[d] = (
                    mine[...].astype(F32) + crossed[d].astype(F32) + came[d].astype(F32)
                ).astype(BF16)

        @pl.when(jnp.logical_not(behind))
        def _():
            going[d] = (mine[...].astype(F32) + crossed[d].astype(F32)).astype(BF16)

        along(up, d).start()

    for d in range(depth - 1, 0, -1):
        pl.when(at.z + d < depth)(lambda: forward(True, d))
        pl.when(at.z >= d)(lambda: forward(False, d))
    across(True, 0).wait_recv()
    total[...] = (
        parts[at.me].astype(F32)
        + across_up[0].astype(F32)
        + (bias_ref[...] - wanted_ref[...].astype(F32))
    )

    @pl.when(at.has_down)
    def _():
        arrived(True, 0)
        total[...] += from_below[0].astype(F32)

    @pl.when(at.has_up)
    def _():
        arrived(False, 0)
        total[...] += from_above[0].astype(F32)

    err = kept_ref[...] * total[...]
    grad[...] = (err / spread_ref[...]).astype(BF16)
    whole[at.me] = grad[...]
    big = Gather(at, grad, whole, big_sems)
    big.start()
    stat[...] = jnp.broadcast_to(jnp.sum(err * err, keepdims=True), stat.shape)
    stats[at.me] = stat[...]
    small = Gather(at, stat, stats, stat_sems)
    small.start()
    for d in range(1, depth):
        big.step(d)
        small.step(d)
    big.finish()
    small.finish()
    for d in range(depth - 1, -1, -1):

        @pl.when(at.z + d < depth)
        def _():
            across(True, d).wait_send()
            if d:
                along(True, d).wait_send()

        if d:

            @pl.when(at.z >= d)
            def _():
                across(False, d).wait_send()
                along(False, d).wait_send()


def to_layer(src, dst, send_sem, recv_sem, layer):
    return pltpu.make_async_remote_copy(
        src_ref=src,
        dst_ref=dst,
        send_sem=send_sem,
        recv_sem=recv_sem,
        device_id={"layer": layer},
        device_id_type=pl.DeviceIdType.MESH,
    )


class Spread:
    def __init__(self, at, ref, sems, pair_sems):
        self.at, self.ref, self.sems, self.pair_sems = at, ref, sems, pair_sems

    def shard_of(self, kind, d, landing=False):
        at = self.at
        shard = at.me - 2 * d if kind in (0, 2) else at.me + 2 * d
        if landing and kind >= 2:
            shard = shard + 1 - 2 * at.y
        return shard

    def hop(self, kind, d):
        at = self.at
        ref = self.ref(self.shard_of(kind, d))
        later = d + 1 if kind < 2 else d
        to = (at.me + 2, at.me - 2, at.partner, at.partner)[kind]
        return send(ref, ref, self.sems.at[0, kind, d], self.sems.at[1, kind, later], to)

    def landing(self, kind, d):
        ref = self.ref(self.shard_of(kind, d, True))
        return send(
            ref, ref, self.sems.at[0, kind, d], self.sems.at[1, kind, d], self.at.partner
        )

    def crossing(self, what, kind, d, act):
        if d != 1 or self.pair_sems is None:
            act(what(kind, d))
            return
        straight = jnp.logical_not(self.at.odd) if kind == 2 else self.at.odd
        pl.when(straight)(lambda: act(what(kind, d)))

    def aside(self, landing=False):
        at = self.at
        ref = self.ref(at.beside + 1 - 2 * at.y if landing else at.partner)
        return send(ref, ref, self.pair_sems.at[0], self.pair_sems.at[1], at.beside)

    def start(self):
        self.hop(2, 0).start()
        pl.when(self.at.has_up)(lambda: self.hop(0, 0).start())
        pl.when(self.at.has_down)(lambda: self.hop(1, 0).start())

    def line(self, d):
        at = self.at

        @pl.when(at.z >= d)
        def _():
            self.landing(0, d).wait_recv()
            pl.when(at.has_up)(lambda: self.hop(0, d).start())
            self.crossing(self.hop, 2, d, lambda one: one.start())

        @pl.when(at.z + d < at.depth)
        def _():
            self.landing(1, d).wait_recv()
            pl.when(at.has_down)(lambda: self.hop(1, d).start())
            self.crossing(self.hop, 3, d, lambda one: one.start())

    def settle(self, d):
        at = self.at
        if d == 0:
            self.landing(2, 0).wait_recv()
            if self.pair_sems is not None:
                self.aside().start()
            return
        if d == 1 and self.pair_sems is not None:
            self.aside(True).wait_recv()
        arrive = lambda one: one.wait_recv()
        pl.when(at.z >= d)(lambda: self.crossing(self.landing, 2, d, arrive))
        pl.when(at.z + d < at.depth)(lambda: self.crossing(self.landing, 3, d, arrive))

    def finish(self):
        at = self.at
        if self.pair_sems is not None:
            self.aside().wait_send()
        for d in range(at.depth):

            @pl.when(at.z >= d)
            def _():
                self.crossing(self.hop, 2, d, lambda one: one.wait_send())
                if d < at.depth - 1:
                    pl.when(at.has_up)(lambda: self.hop(0, d).wait_send())

            @pl.when(at.z + d < at.depth)
            def _():
                if d > 0:
                    self.crossing(self.hop, 3, d, lambda one: one.wait_send())
                if d < at.depth - 1:
                    pl.when(at.has_down)(lambda: self.hop(1, d).wait_send())


def advance(at, *stages):
    for group, d, use in stages:
        if 0 < d < at.depth:
            for one in group:
                one.line(d)
    for group, d, use in stages:
        if d == 0:
            for one in group:
                one.start()
    for group, d, use in stages:
        if d == 1:
            use(at.me)
        if 0 < d < at.depth:
            both_ways(at, at.me, d, use)
    for group, d, use in stages:
        if d > 0:
            for one in group:
                one.settle(d - 1)
    for group, d, use in stages:
        if d == 1:
            use(at.partner)
        if d > 1:
            both_ways(at, at.partner, d - 1, use)


def reaches(at, step):
    return jnp.logical_and(at.z + step >= 0, at.z + step < at.depth)


def both_ways(at, start, d, use):
    @pl.loop(0, 2)
    def _(row):
        step = (1 - 2 * row) * d
        pl.when(reaches(at, step))(lambda: use(start + 2 * step))


def step_kernel(
    lat_count,
    own,
    wanted_ref,
    enc_weight,
    enc_bias,
    gate_ref,
    dec_weight,
    dec_bias,
    ids_ref,
    turned_x_out,
    grads_out,
    acts_out,
    own_term_out,
    terms_out,
    loss,
    whole_x,
    turned_x,
    wanted_here,
    gate_here,
    enc_blocks,
    acc_enc,
    acts,
    turned,
    blocks,
    base,
    kept,
    leaving,
    crossed,
    came,
    going,
    pair_in,
    fresh,
    whole_g,
    column,
    acc,
    giving,
    given,
    terms,
    losses,
    spread_tile,
    stats,
    x_sems,
    x_pair_sems,
    g_sems,
    g_pair_sems,
    across_sems,
    line_sems,
    pair_sems,
    layer_sems,
    mate_sems,
    loss_sems,
    stat_sems,
    enc_sems,
    block_sems,
    local_sems,
    out_sems,
):
    at = Place(lat_count)
    at.odd = at.z % 2 == 1
    at.beside = at.me + 2 - 4 * (at.z % 2)
    depth = at.depth
    layer_count = acts.shape[1]
    rows, half = whole_x.shape[2:]
    piece = half // 2
    layer = lax.axis_index("layer")
    pairs = layer_count // 2
    pair, core = layer // 2, layer % 2
    mate = layer + 1 - 2 * core
    cells = lat_count * rows * half * 2

    def own_half(h):
        return pltpu.make_async_copy(
            own.at[:, pl.ds(h * half, half)], whole_x.at[h, at.me], local_sems.at[h]
        )

    def load_enc(g):
        return pltpu.make_async_copy(
            enc_weight.at[:, pl.ds(g * rows, rows)], enc_blocks.at[g], enc_sems.at[g]
        )

    def load_dec(g):
        return pltpu.make_async_copy(
            dec_weight.at[:, :, pl.ds(g * rows, rows)], blocks.at[g], block_sems.at[g]
        )

    fetch = pltpu.make_async_copy(wanted_ref, wanted_here, local_sems.at[2])
    fetch_gate = pltpu.make_async_copy(gate_ref, gate_here, local_sems.at[3])
    own_half(0).start()
    own_half(1).start()
    for g in range(lat_count):
        load_enc(g).start()
    fetch.start()
    fetch_gate.start()

    barrier = pltpu.get_barrier_semaphore()
    for k in range(1, layer_count):
        other = lax.rem(layer + k, layer_count)
        pl.semaphore_signal(
            barrier, inc=1, device_id={"layer": other}, device_id_type=pl.DeviceIdType.MESH
        )
    own_half(0).wait()
    own_half(1).wait()
    greet(at, layer_count - 1)

    def tally(which):
        return Spread(at, lambda shard: stats.at[which, shard], stat_sems.at[which], None)

    def feature_piece(h, q):
        def ref(shard):
            return whole_x.at[h, shard, pl.ds(q * (rows // 2), rows // 2)]

        return Spread(at, ref, x_sems.at[h, q], x_pair_sems.at[h] if q else None)

    def use_x(h):
        def use(g):
            acc_enc[h] += jnp.dot(enc_blocks[g], whole_x[h, g], preferred_element_type=F32)

        return use

    gather_x = [[feature_piece(h, q) for q in range(2)] for h in range(2)]
    gather_x.append([tally(0)])

    def stage_x(*which):
        uses = use_x(0), use_x(1), lambda g: None
        advance(at, *[(gather_x[h], d, uses[h]) for h, d in which])

    stage_x((0, 0))
    bias = jnp.transpose(jnp.broadcast_to(enc_bias[...].astype(F32), (half, enc_bias.shape[1])))
    acc_enc[0] = bias
    acc_enc[1] = bias
    turned[...] = jnp.zeros_like(turned)
    for g in range(lat_count):
        load_enc(g).wait()
    for g in range(lat_count):
        load_dec(g).start()
    stage_x((0, 1), (1, 0))
    fetch.wait()
    wanted = wanted_here[...].astype(F32)
    centered = wanted - jnp.mean(wanted, axis=1, keepdims=True)
    total = jnp.sum(centered * centered, keepdims=True)
    stats[0, at.me] = jnp.broadcast_to(total, stats.shape[2:])
    stage_x((0, 2), (1, 1), (2, 0))
    stage_x((0, 3), (1, 2), (2, 1))
    base[...] = dec_bias[...].astype(F32) - jnp.transpose(wanted_here[...].astype(F32))
    fetch_gate.wait()
    stage_x((0, 4), (2, 2))

    def over(h, k):
        ref = acts.at[h, layer]
        return to_layer(
            ref, ref, layer_sems.at[0, h, 0, k], layer_sems.at[1, h, 0, k], layer + 2 * k
        )

    def pass_on(h, k):
        ref = acts.at[h, layer - 2 * k]
        return to_layer(ref, ref, layer_sems.at[0, h, 1, k], layer_sems.at[1, h, 1, k], mate)

    def landed(h, kind, k):
        ref = acts.at[h, layer - 2 * k if kind == 0 else mate - 2 * k]
        sem = layer_sems.at[1, h, kind, k]
        return to_layer(ref, ref, layer_sems.at[0, h, kind, k], sem, mate)

    def turn(h, source):
        turned[source, h * half : (h + 1) * half] = jnp.transpose(acts[h, source])

    def exchange(h):
        gate = gate_here[:, h * half : (h + 1) * half].astype(F32)
        acts[h, layer] = (gate * acc_enc[h]).astype(BF16)
        for k in range(1, pairs):
            pl.when(pair + k < pairs)(lambda: over(h, k).start())
        pl.when(core == 0)(lambda: pass_on(h, 0).start())
        turn(h, layer)
        yield
        for k in range(1, pairs):

            @pl.when(pair >= k)
            def _():
                landed(h, 0, k).wait_recv()
                pass_on(h, k).start()
                turn(h, layer - 2 * k)

        yield

        @pl.when(core == 1)
        def _():
            landed(h, 1, 0).wait_recv()
            turn(h, mate)

        for k in range(1, pairs):

            @pl.when(pair >= k)
            def _():
                landed(h, 1, k).wait_recv()
                turn(h, mate - 2 * k)

        yield

    def exchange_sent(h):
        pl.when(core == 0)(lambda: pass_on(h, 0).wait_send())
        for k in range(1, pairs):
            pl.when(pair >= k)(lambda: pass_on(h, k).wait_send())
            pl.when(pair + k < pairs)(lambda: over(h, k).wait_send())

    moves = [exchange(h) for h in range(2)]
    next(moves[0])
    stage_x((1, 3), (2, 3))
    next(moves[0])
    stage_x((1, 4), (2, 4))
    next(moves[1])
    next(moves[0])
    for g in range(lat_count):
        load_dec(g).wait()
    spread_tile[...] = jnp.sum(stats[0], axis=0) / cells + EPSILON
    spread = jnp.max(spread_tile[...], keepdims=True)

    def part(h, g):
        some = slice(h * half, (h + 1) * half)
        got = jnp.dot(turned[0, some], blocks[g, 0], preferred_element_type=F32)
        for source in range(1, layer_count):
            got += jnp.dot(turned[source, some], blocks[g, source], preferred_element_type=F32)
        fresh[...] = got

    def within(p):
        return pl.ds(p % 2 * piece, piece)

    def of(p):
        return pl.ds(p * piece, piece)

    def across(p, row, d):
        return send(
            leaving.at[row, d, of(p)],
            crossed.at[row, d, of(p)],
            across_sems.at[0, p, row, d],
            across_sems.at[1, p, row, d],
            at.partner,
        )

    def aside(p, row):
        return send(
            leaving.at[row, 1, of(p)],
            pair_in.at[p // 2],
            pair_sems.at[0, p // 2],
            pair_sems.at[1, p // 2],
            at.beside,
        )

    def by_side(p, row, d, cross, turn_aside=None):
        if d != 1 or p % 2 == 0:
            cross()
            return
        beside = lax.rem(at.z + row, 2) == 0
        pl.when(jnp.logical_not(beside))(cross)
        if turn_aside is not None:
            pl.when(beside)(turn_aside)

    def along(p, row, d):
        return send(
            going.at[row, d, of(p)],
            came.at[row, d - 1, of(p)],
            line_sems.at[0, p, row, d],
            line_sems.at[1, p, row, d - 1],
            at.me + 2 - 4 * row,
        )

    def arrived(p, row, d):
        ref = came.at[row, d, of(p)]
        sems = line_sems.at[0, p, row, d], line_sems.at[1, p, row, d]
        send(ref, ref, *sems, at.partner).wait_recv()
        fresh[within(p), :] += came[row, d, of(p)].astype(F32)

    def met(p, row, d):
        across(p, row, d).wait_recv()
        fresh[within(p), :] += crossed[row, d, of(p)].astype(F32)

    def leave(h, row, d):
        part(h, at.partner + 2 * d * (1 - 2 * row))
        if d == 0:
            aside(2 * h + 1, 0).wait_recv()
            fresh[piece:] += pair_in[h].astype(F32)
        leaving[row, d, h * half : (h + 1) * half] = fresh[...].astype(BF16)
        for p in (2 * h, 2 * h + 1):
            by_side(
                p, row, d, lambda: across(p, row, d).start(), lambda: aside(p, row).start()
            )

    def leaves(h, d):
        if d == 0:
            leave(h, 0, 0)
            return

        @pl.loop(0, 2)
        def _(row):
            pl.when(reaches(at, d * (1 - 2 * row)))(lambda: leave(h, row, d))

    def forward(h, row, d):
        part(h, at.me + 2 * d * (1 - 2 * row))
        for p in (2 * h, 2 * h + 1):
            by_side(p, row, d, lambda: met(p, row, d))
            if d < depth - 1:
                pl.when(reaches(at, 2 * row - 1))(lambda: arrived(p, row, d))
            going[row, d, of(p)] = fresh[within(p), :].astype(BF16)
            along(p, row, d).start()

    def forwards(h, d):
        @pl.loop(0, 2)
        def _(row):
            pl.when(reaches(at, d * (1 - 2 * row)))(lambda: forward(h, row, d))

    def token_piece(p):
        def ref(shard):
            return whole_g.at[shard, of(p)]

        return Spread(at, ref, g_sems.at[p], g_pair_sems.at[p // 2] if p % 2 else None)

    gather_g = [token_piece(p) for p in range(4)]
    gather_g.append(tally(1))

    def use_g(g):
        column[...] = jnp.transpose(whole_g[g])
        for source in range(layer_count):
            acc[source] += jnp.dot(blocks[g, source], column[...], preferred_element_type=F32)

    def close(h):
        part(h, at.me)
        fresh[...] += base[h * half : (h + 1) * half]
        for p in (2 * h, 2 * h + 1):
            met(p, 0, 0)
            pl.when(at.has_down)(lambda: arrived(p, 0, 0))
            pl.when(at.has_up)(lambda: arrived(p, 1, 0))
            err = kept[of(p), :1] * fresh[within(p), :]
            whole_g[at.me, of(p)] = (err / spread).astype(BF16)
            gather_g[p].start()
            total = jnp.sum(err * err, keepdims=True)
            if p == 0:
                stats[1, at.me] = jnp.broadcast_to(total, stats.shape[2:])
            else:
                stats[1, at.me] += total
        if h:
            gather_g[4].start()

    def turn_x(g):
        for h in range(2):
            turned_x[g, h * half : (h + 1) * half] = jnp.transpose(whole_x[h, g])

    def stage_g(*which):
        uses = turn_x, use_g
        advance(at, *[(gather_g[2 * h : 2 * h + 2 + h], d, uses[h]) for h, d in which])

    leaves(0, 3)
    leaves(0, 2)
    leaves(0, 1)
    next(moves[1])
    forwards(0, 3)
    next(moves[1])
    leaves(1, 3)
    forwards(0, 2)
    leaves(1, 2)
    leaves(0, 0)
    forwards(0, 1)
    leaves(1, 1)
    forwards(1, 3)
    ids = jnp.broadcast_to((ids_ref[...] != 128000).astype(F32), (128, 2 * half))
    kept[...] = jnp.transpose(ids)
    close(0)
    forwards(1, 2)
    stage_g((0, 1))
    leaves(1, 0)
    forwards(1, 1)
    stage_g((0, 2))
    acc[...] = jnp.zeros_like(acc)
    close(1)
    stage_g((0, 3), (1, 1))
    stage_g((0, 4), (1, 2))
    stage_g((1, 3))

    def out(which):
        src, dst = (
            (turned_x, turned_x_out),
            (acts, acts_out),
            (whole_g, grads_out),
            (acc.at[layer], own_term_out),
            (terms, terms_out),
        )[which]
        return pltpu.make_async_copy(src, dst, out_sems.at[which])

    out(0).start()
    out(1).start()
    stage_g((1, 4))
    out(2).start()
    losses[layer] = jnp.sum(stats[1], axis=0) / (2.0 * spread_tile[...] * cells)

    def tell(k, told=False):
        other = lax.rem(layer + (layer_count - k if told else k), layer_count)
        ref = losses.at[other if told else layer]
        return to_layer(ref, ref, loss_sems.at[0, k], loss_sems.at[1, k], other)

    def give(k):
        return to_layer(
            giving.at[k], given.at[k], mate_sems.at[0, k], mate_sems.at[1, k], mate
        )

    def hand(k):
        giving[k] = acc[mate - 2 * k].astype(BF16)
        give(k).start()

    for k in range(pairs - 1, 0, -1):
        pl.when(pair >= k)(lambda: hand(k))
    pl.when(core == 1)(lambda: hand(0))
    for k in range(1, layer_count):
        tell(k).start()
    for k in range(pairs - 1, 0, -1):

        @pl.when(pair >= k)
        def _():
            give(k).wait_recv()
            terms[k - 1] = (acc[layer - 2 * k] + given[k].astype(F32)).astype(BF16)
            give(k).wait_send()

        @pl.when(pair < k)
        def _():
            terms[k - 1] = jnp.zeros(terms.shape[1:], BF16)

    out(4).start()

    @pl.when(core == 0)
    def _():
        give(0).wait_recv()
        acc[layer] += given[0].astype(F32)

    out(3).start()
    pl.when(core == 1)(lambda: give(0).wait_send())
    for k in range(1, layer_count):
        tell(k, True).wait_recv()
        tell(k).wait_send()
    loss[...] = jnp.sum(losses[...], axis=0)[:1, :1]
    for group in gather_x:
        for one in group:
            one.finish()
    for h in range(2):
        exchange_sent(h)
    for one in gather_g:
        one.finish()
    for p in range(4):
        if p % 2:
            aside(p, 0).wait_send()
        for d in range(depth):
            for row in range(2):
                if d or row == 0:

                    @pl.when(reaches(at, d * (1 - 2 * row)))
                    def _():
                        by_side(p, row, d, lambda: across(p, row, d).wait_send())
                        if d:
                            along(p, row, d).wait_send()

    for which in range(5):
        out(which).wait()


VMEM = pl.BlockSpec(memory_space=pltpu.VMEM)
HBM = pl.BlockSpec(memory_space=pltpu.HBM)


def step(inputs_local, wanted, enc_weight, enc_bias, gate, dec_weight, dec_bias, ids, lat_count):
    rows, tokens = inputs_local.shape
    layer_count, lat_rows, _ = dec_weight.shape
    depth = lat_count // 2
    pairs = layer_count // 2
    half = tokens // 2
    slots = pltpu.VMEM((2, depth, tokens, rows), BF16)
    dma = pltpu.SemaphoreType.DMA
    return pl.pallas_call(
        functools.partial(step_kernel, lat_count),
        out_shape=(
            jax.ShapeDtypeStruct((lat_count, tokens, rows), BF16),
            jax.ShapeDtypeStruct((lat_count, tokens, rows), BF16),
            jax.ShapeDtypeStruct((2, layer_count, lat_rows, half), BF16),
            jax.ShapeDtypeStruct((lat_rows, tokens), F32),
            jax.ShapeDtypeStruct((pairs - 1, lat_rows, tokens), BF16),
            jax.ShapeDtypeStruct((1, 1), F32),
        ),
        in_specs=[HBM, HBM, HBM, VMEM, HBM, HBM, VMEM, VMEM],
        out_specs=(HBM,) * 5 + (VMEM,),
        scratch_shapes=[
            pltpu.VMEM((2, lat_count, rows, half), BF16),
            pltpu.VMEM((lat_count, tokens, rows), BF16),
            pltpu.VMEM((rows, tokens), BF16),
            pltpu.VMEM((lat_rows, tokens), jnp.int32),
            pltpu.VMEM((lat_count, lat_rows, rows), BF16),
            pltpu.VMEM((2, lat_rows, half), F32),
            pltpu.VMEM((2, layer_count, lat_rows, half), BF16),
            pltpu.VMEM((layer_count, tokens, lat_rows), BF16),
            pltpu.VMEM((lat_count, layer_count, lat_rows, rows), BF16),
            pltpu.VMEM((tokens, rows), F32),
            pltpu.VMEM((tokens, 128), F32),
        ]
        + [slots] * 4
        + [
            pltpu.VMEM((2, half // 2, rows), BF16),
            pltpu.VMEM((half, rows), F32),
            pltpu.VMEM((lat_count, tokens, rows), BF16),
            pltpu.VMEM((rows, tokens), BF16),
            pltpu.VMEM((layer_count, lat_rows, tokens), F32),
            pltpu.VMEM((pairs, lat_rows, tokens), BF16),
            pltpu.VMEM((pairs, lat_rows, tokens), BF16),
            pltpu.VMEM((pairs - 1, lat_rows, tokens), BF16),
            pltpu.VMEM((layer_count, 8, 128), F32),
            pltpu.VMEM((8, 128), F32),
            pltpu.VMEM((2, lat_count, 8, 128), F32),
            dma((2, 2, 2, 4, depth + 1)),
            dma((2, 2)),
            dma((4, 2, 4, depth + 1)),
            dma((2, 2)),
            dma((2, 4, 2, depth)),
            dma((2, 4, 2, depth)),
            dma((2, 2)),
            dma((2, 2, 2, pairs)),
            dma((2, pairs)),
            dma((2, layer_count)),
            dma((2, 2, 4, depth + 1)),
            dma((lat_count,)),
            dma((lat_count,)),
            dma((4,)),
            dma((5,)),
        ],
        compiler_params=pltpu.CompilerParams(
            collective_id=2, has_side_effects=True, vmem_limit_bytes=60 << 20
        ),
    )(inputs_local, wanted, enc_weight, enc_bias, gate, dec_weight, dec_bias, ids)


def dec_grad_kernel(acts_ref, grads_ref, out, acts, grads, ring, in_sems, out_sems):
    layer = lax.axis_index("layer")
    slots, block, _ = ring.shape
    _, layer_count, lat_rows, _ = acts.shape
    lat_count, _, rows = grads.shape
    parts = lat_rows // block
    count = layer_count * parts
    def fetch_acts(source):
        return pltpu.make_async_copy(
            acts_ref.at[:, source], acts.at[:, source], in_sems.at[lat_count + source]
        )

    def fetch_grads(g):
        return pltpu.make_async_copy(grads_ref.at[g], grads.at[g], in_sems.at[g])

    fetch_acts(0).start()
    for g in range(lat_count):
        fetch_grads(g).start()
    for source in range(1, layer_count):
        fetch_acts(source).start()
    fetch_acts(0).wait()

    def write(i):
        here = pl.ds(lax.rem(i, parts) * block, block)
        slot = lax.rem(i, slots)
        return pltpu.make_async_copy(
            ring.at[slot], out.at[lax.div(i, parts), here], out_sems.at[slot]
        )

    def made(i, g):
        source, here = lax.div(i, parts), pl.ds(lax.rem(i, parts) * block, block)
        left = jnp.concatenate([acts[0, source, here], acts[1, source, here]], axis=1)
        return jnp.dot(left, grads[g], preferred_element_type=F32).astype(BF16)

    for g in range(lat_count):
        if g % (lat_count // 2) == 0:
            for later in range(g, g + lat_count // 2):
                fetch_grads(later).wait()
        ring[0, :, g * rows : (g + 1) * rows] = made(0, g)
    write(0).start()
    for source in range(1, layer_count):
        fetch_acts(source).wait()

    @pl.loop(1, count)
    def _(i):
        pl.when(i >= slots)(lambda: write(i - slots).wait())
        source, slot = lax.div(i, parts), lax.rem(i, slots)

        @pl.when(source <= layer)
        def _():
            for g in range(lat_count):
                ring[slot, :, g * rows : (g + 1) * rows] = made(i, g)

        @pl.when(source > layer)
        def _():
            ring[slot] = jnp.zeros(ring.shape[1:], BF16)

        write(i).start()

    for i in range(max(count - slots, 0), count):
        write(i).wait()


def dec_grad(acts, grads):
    _, layer_count, lat_rows, half = acts.shape
    lat_count, tokens, rows = grads.shape
    features = lat_count * rows
    block = lat_rows // 2
    return pl.pallas_call(
        dec_grad_kernel,
        out_shape=jax.ShapeDtypeStruct((layer_count, lat_rows, features), BF16),
        in_specs=[HBM, HBM],
        out_specs=HBM,
        scratch_shapes=[
            pltpu.VMEM(acts.shape, BF16),
            pltpu.VMEM(grads.shape, BF16),
            pltpu.VMEM((3, block, features), BF16),
            pltpu.SemaphoreType.DMA((lat_count + layer_count,)),
            pltpu.SemaphoreType.DMA((3,)),
        ],
        cost_estimate=pl.CostEstimate(
            flops=2 * layer_count * lat_rows * tokens * features,
            bytes_accessed=2 * layer_count * lat_rows * features,
            transcendentals=0,
        ),
        compiler_params=pltpu.CompilerParams(vmem_limit_bytes=60 << 20),
    )(acts, grads)


def enc_grad_kernel(term, came, gate, inputs, out):
    total = term[...]
    for k in range(came.shape[0]):
        total = total + came[k].astype(F32)
    left = (gate[...].astype(F32) * total).astype(BF16)
    lat_count, _, rows = inputs.shape
    for g in range(lat_count):
        made = jnp.dot(left, inputs[g], preferred_element_type=F32)
        out[:, g * rows : (g + 1) * rows] = made.astype(BF16)


def enc_grad(term, came, gate, inputs):
    lat_rows, tokens = term.shape
    lat_count, _, rows = inputs.shape
    block = lat_rows // 4
    return pl.pallas_call(
        enc_grad_kernel,
        grid=(4,),
        out_shape=jax.ShapeDtypeStruct((lat_rows, lat_count * rows), BF16),
        in_specs=[
            pl.BlockSpec((block, tokens), lambda r: (r, 0)),
            pl.BlockSpec((came.shape[0], block, tokens), lambda r: (0, r, 0)),
            pl.BlockSpec((block, tokens), lambda r: (r, 0)),
            pl.BlockSpec(inputs.shape, lambda r: (0, 0, 0)),
        ],
        out_specs=pl.BlockSpec((block, lat_count * rows), lambda r: (r, 0)),
        compiler_params=pltpu.CompilerParams(vmem_limit_bytes=32 << 20),
    )(term, came, gate, inputs)


def gather_inputs(inputs_local, wanted, lat_count):
    rows, tokens = inputs_local.shape
    depth = lat_count // 2
    return pl.pallas_call(
        functools.partial(gather_kernel, lat_count),
        out_shape=(
            jax.ShapeDtypeStruct((lat_count, rows, tokens), BF16),
            jax.ShapeDtypeStruct((lat_count, 8, 128), F32),
        ),
        in_specs=[VMEM] * 2,
        out_specs=(VMEM, VMEM),
        scratch_shapes=[
            pltpu.VMEM((8, 128), F32),
            pltpu.SemaphoreType.DMA((2, 4, depth + 1)),
            pltpu.SemaphoreType.DMA((2, 4, depth + 1)),
            pltpu.SemaphoreType.DMA,
        ],
        compiler_params=pltpu.CompilerParams(
            collective_id=0, has_side_effects=True, vmem_limit_bytes=32 << 20
        ),
    )(inputs_local, wanted)


def reduce_and_gather(parts, wanted, bias, kept, spread, lat_count):
    _, rows, tokens = parts.shape
    depth = lat_count // 2
    slots = pltpu.VMEM((depth, rows, tokens), BF16)
    return pl.pallas_call(
        functools.partial(reduce_kernel, lat_count),
        out_shape=(
            jax.ShapeDtypeStruct((lat_count, rows, tokens), BF16),
            jax.ShapeDtypeStruct((lat_count, 8, 128), F32),
        ),
        in_specs=[VMEM] * 5,
        out_specs=(VMEM, VMEM),
        scratch_shapes=[slots] * 6
        + [
            pltpu.VMEM((rows, tokens), F32),
            pltpu.VMEM((rows, tokens), BF16),
            pltpu.VMEM((8, 128), F32),
            pltpu.SemaphoreType.DMA((2, 2, depth)),
            pltpu.SemaphoreType.DMA((2, 2, depth)),
            pltpu.SemaphoreType.DMA((2, 4, depth + 1)),
            pltpu.SemaphoreType.DMA((2, 4, depth + 1)),
        ],
        compiler_params=pltpu.CompilerParams(
            collective_id=1, has_side_effects=True, vmem_limit_bytes=40 << 20
        ),
    )(parts, wanted, bias, kept, spread)


def on_device(
    resid_in, resid_out, token_ids, active_mask, enc_weight, enc_bias, dec_weight, dec_bias
):
    layer_count = lax.axis_size("layer")
    lat_count = lax.axis_size("lat")
    lat_rows = enc_weight.shape[1]
    feature_rows, token_count = resid_in.shape[1:]
    fused = feature_rows % 128 == 0 and lat_rows % 128 == 0 and token_count == 256
    fused = fused and layer_count % 2 == 0 and layer_count > 2 and lat_count == 8
    args = (
        resid_in, resid_out, token_ids, active_mask, enc_weight, enc_bias, dec_weight, dec_bias
    )
    return fused_step(*args) if fused else plain_step(*args)


def fused_step(
    resid_in, resid_out, token_ids, active_mask, enc_weight, enc_bias, dec_weight, dec_bias
):
    layer_count = lax.axis_size("layer")
    pairs = layer_count // 2
    inputs, grads, acts, own_term, terms, loss_tile = step(
        resid_in[0],
        resid_out[0],
        enc_weight[0],
        enc_bias,
        active_mask[0],
        dec_weight[0],
        dec_bias,
        token_ids[None, :],
        lax.axis_size("lat"),
    )
    came = [
        lax.ppermute(
            terms[k - 1], "layer", [(d, d - 2 * k) for d in range(2 * k, layer_count)]
        )[None]
        for k in range(1, pairs)
    ]
    came = came[0] if pairs == 2 else jnp.concatenate(came, axis=0)
    dec_out = dec_grad(acts, grads)
    enc_out = enc_grad(own_term, came, active_mask[0], inputs)
    return (enc_out[None], dec_out[None], loss_tile.reshape(()))


def plain_step(
    resid_in, resid_out, token_ids, active_mask, enc_weight, enc_bias, dec_weight, dec_bias
):
    layer_count = lax.axis_size("layer")
    lat_count = lax.axis_size("lat")
    layer_here = lax.axis_index("layer")
    inputs_local = resid_in[0]
    wanted = resid_out[0]
    weight_enc = enc_weight[0]
    lat_rows = weight_enc.shape[0]
    feature_count = weight_enc.shape[1]
    feature_rows, token_count = inputs_local.shape
    total_cells = feature_count * token_count
    kept_tokens = (token_ids != 128000).astype(F32)
    source_ids = jnp.arange(layer_count)
    gating = active_mask[0].astype(F32)
    weight_rows = dec_weight[0].reshape(layer_count * lat_rows, feature_count)
    whole_inputs, target_stats = gather_inputs(inputs_local, wanted, lat_count)
    whole_inputs = whole_inputs.reshape(feature_count, token_count)
    spread = jnp.sum(target_stats[:, 0, 0]) / total_cells + EPSILON
    preact = jnp.dot(weight_enc, whole_inputs, preferred_element_type=F32)
    preact = preact + enc_bias[0].astype(F32)[:, None]
    latents = (gating * preact).astype(BF16)
    gathered = lax.all_gather(latents[None], "layer", axis=0, tiled=True)
    acts_stack = jnp.where(
        (source_ids <= layer_here)[:, None, None], gathered, jnp.zeros((), BF16)
    )
    stack_rows = acts_stack.reshape(layer_count * lat_rows, token_count)
    parts = lax.dot_general(
        weight_rows, stack_rows, (((0,), (0,)), ((), ())), preferred_element_type=F32
    ).astype(BF16)
    full_grad, err_stats = reduce_and_gather(
        parts.reshape(lat_count, feature_rows, token_count),
        wanted,
        dec_bias[0].astype(F32)[:, None],
        kept_tokens[None, :],
        jnp.broadcast_to(spread, (1, token_count)),
        lat_count,
    )
    full_grad = full_grad.reshape(feature_count, token_count)
    layer_loss = jnp.sum(err_stats[:, 0, 0]) / (2.0 * spread * total_cells)
    total_loss = lax.psum(layer_loss, "layer")
    grad_rows = jnp.dot(weight_rows, full_grad, preferred_element_type=F32).reshape(
        layer_count, lat_rows, token_count
    )
    grad_rows = (grad_rows * (source_ids <= layer_here).astype(F32)[:, None, None]).astype(BF16)
    dec_out = lax.dot_general(
        stack_rows, full_grad, (((1,), (1,)), ((), ())), preferred_element_type=F32
    )
    dec_out = dec_out.astype(BF16).reshape(1, layer_count, lat_rows, feature_count)
    latent_grad = lax.psum_scatter(grad_rows, "layer", scatter_dimension=0, tiled=True)[0]
    preact_grad = (gating * latent_grad.astype(F32)).astype(BF16)
    enc_out = lax.dot_general(
        preact_grad, whole_inputs, (((1,), (1,)), ((), ())), preferred_element_type=F32
    )
    return (enc_out.astype(BF16)[None], dec_out, total_loss)


def solution(mesh):
    in_specs = (
        P("layer", "lat", None),
        P("layer", "lat", None),
        P(),
        P("layer", "lat", None),
        P("layer", "lat", None),
        P("layer", "lat"),
        P("layer", None, "lat", None),
        P("layer", "lat"),
    )
    out_specs = (P("layer", "lat", None), P("layer", None, "lat", None), P())
    return jax.shard_map(
        on_device, mesh=mesh, in_specs=in_specs, out_specs=out_specs, check_vma=False
    )
```
